32 devices in a mesh: clips: 2 (over y), ctx: 4 (over z), head: 4 (over x, core).
Axes of the slice: x: 2, y: 2, z: 4, core: 2. Of those that a mesh axis runs over, the one named last changes fastest.
Arguments:
- queries: bfloat16 [9216, 1536], P(('clips', 'ctx', 'head')), parts along dimension 0
- keys: bfloat16 [9216, 1536], P(('clips', 'ctx', 'head')), parts along dimension 0
- values: bfloat16 [9216, 1536], P(('clips', 'ctx', 'head')), parts along dimension 0, may hold values from -4.5 to 4.5
- neighbors: int32 [24, 8], P(('clips', 'ctx')), parts along dimension 0, may hold values from 0 to 11, as said below
- tile_counts: int32 [24], P(('clips', 'ctx')), parts along dimension 0, may hold values from 192 to 384
Outputs:
- attended: bfloat16 [9216, 1536], P(('clips', 'ctx', 'head')), parts along dimension 0
The draws below stay inside these ranges and needn't reach their ends.
There are 2 independent parts, one for each index of `clips`. The reference program is written for one: setup_inputs(seed, part) draws one part's arguments, and reference() takes and returns one part's arrays. A program takes and returns all parts, laid end to end along the dimension named above; each array names one. Nothing has to cross between parts.
Inputs may be any that keep to these rules, and one draw needn't show every extreme that they name: `neighbors`: row t starts with t itself, followed by 8 - 1 distinct other tiles of t's 3 x 3 x 3 window of tiles: frame layer, row and column each differ from t's by at most one.
All inputs are finite; a program needn't handle non-finite values.
Results may differ from the reference program's by a relative error of at most 0.0049.
Values may be sent and summed in bfloat16 or wider, within the bound.
A program may use at most 64 MiB of HBM per device.

```python
import jax
import jax.numpy as jnp
from jax import lax

HEADS = 12
DH = 128
TILE = 384
TH = 2
TW = 3
NB = 8
NT = 12
TOKENS = 4608


def base_field(key):
    return jax.random.truncated_normal(key, -4.5, 4.5, (TOKENS, HEADS * DH), jnp.float32)


def draw_keys(key, part):
    field = base_field(jax.random.fold_in(key, 7))
    return field.astype(jnp.bfloat16)


def draw_queries(key, part):
    field = base_field(jax.random.fold_in(key, 9))
    return field.astype(jnp.bfloat16)


def draw_neighbors(key, part):
    layer_size = TH * TW
    layers = NT // layer_size
    tile_ids = jnp.arange(NT, dtype=jnp.int32)
    frame = tile_ids // layer_size
    row_pos = tile_ids // TW % TH
    col_pos = tile_ids % TW
    cube = jnp.concatenate([jnp.arange(13, dtype=jnp.int32), jnp.arange(14, 27, dtype=jnp.int32)])
    step_frame = cube // 9 - 1
    step_row = cube // 3 % 3 - 1
    step_col = cube % 3 - 1
    cand_frame = frame[:, None] + step_frame[None, :]
    cand_row = row_pos[:, None] + step_row[None, :]
    cand_col = col_pos[:, None] + step_col[None, :]
    in_range = (cand_frame >= 0) & (cand_frame < layers) & (cand_row >= 0) & (cand_row < TH) & (cand_col >= 0) & (cand_col < TW)
    candidates = cand_frame * layer_size + cand_row * TW + cand_col
    priority = jax.vmap(lambda sub_key: jax.random.permutation(sub_key, 26))(jax.random.split(jax.random.fold_in(key, 5), NT))
    priority = priority + jnp.where(in_range, 0, 1000)
    ranking = jnp.argsort(priority, axis=1, stable=True)
    chosen = jnp.take_along_axis(candidates, ranking, axis=1)[:, :NB - 1]
    return jnp.concatenate([tile_ids[:, None], chosen], axis=1).astype(jnp.int32)


def draw_tile_counts(key, part):
    ragged = jax.random.randint(jax.random.fold_in(key, 1), (NT,), 0, 4) == 0
    shorter = jax.random.randint(jax.random.fold_in(key, 2), (NT,), TILE // 2, TILE)
    counts_all = jnp.where(ragged, shorter, TILE)
    counts_all = counts_all.at[0].set(TILE).at[1].set(TILE // 2)
    return counts_all.astype(jnp.int32)


def level_of(stream_key, shape, shards, least, top_value):
    def one(position, shards_of):
        draws = jax.random.uniform(jax.random.fold_in(jax.random.fold_in(stream_key, 6), position), (shards_of,), jnp.float32, least / len(shards), top_value / len(shards))
        return jnp.repeat(jnp.exp(draws), shape[position] // shards_of).reshape((-1,) + (1,) * (len(shape) - position - 1))

    loudness = one(*shards[0])
    for cut in shards[1:]:
        loudness = loudness * one(*cut)
    return loudness


def noise(stream_key, dims, scale, reach, cuts=(), held_as=jnp.bfloat16):
    values = jax.random.normal(stream_key, dims, jnp.float32) * scale
    if len(cuts) > 0:
        values = level_of(stream_key, dims, cuts, -0.22, 0.18) * values
    return jnp.clip(values, min=-reach, max=reach).astype(held_as)


def setup_inputs(seed: int = 0, part: int = 0) -> dict:
    splits = jax.random.split(jax.random.key(seed), 6)
    part_keys = jax.random.split(jax.random.fold_in(splits[5], part), 6)
    return {
        "queries": draw_queries(jax.random.fold_in(jax.random.fold_in(splits[5], part), 71), part),
        "keys": draw_keys(jax.random.fold_in(jax.random.fold_in(splits[5], part), 71), part),
        "values": noise(part_keys[2], (TOKENS, HEADS * DH), 1.0, 4.5, ((0, 16),)),
        "neighbors": draw_neighbors(jax.random.fold_in(jax.random.fold_in(splits[5], part), 71), part),
        "tile_counts": draw_tile_counts(jax.random.fold_in(jax.random.fold_in(splits[5], part), 71), part),
    }


def attend_tile(query_tile, key_rows, value_rows, key_mask):
    scores = jnp.einsum("qhd,khd->hqk", query_tile.astype(jnp.float32), key_rows.astype(jnp.float32)) * (DH ** -0.5)
    scores = jnp.where(key_mask[None, None, :], scores, -jnp.inf)
    highest = jnp.max(scores, axis=2, keepdims=True)
    weights = jnp.exp(scores - highest)
    totals = jnp.sum(weights, axis=2, keepdims=True)
    rounded = lax.optimization_barrier(weights.astype(jnp.bfloat16))
    summed = jnp.einsum("hqk,khd->qhd", rounded.astype(jnp.float32), value_rows.astype(jnp.float32))
    return (summed / jnp.transpose(totals, (1, 0, 2))).astype(jnp.bfloat16)


def reference(queries, keys, values, neighbors, tile_counts):
    query_tiles = queries.reshape(NT, TILE, HEADS, DH)
    key_tiles = keys.reshape(NT, TILE, HEADS, DH)
    value_tiles = values.reshape(NT, TILE, HEADS, DH)
    slot_index = jnp.arange(TILE, dtype=jnp.int32)

    def one_tile(tile_id):
        listed = neighbors[tile_id]
        listed_live = listed >= 0
        safe_ids = jnp.maximum(listed, 0).astype(jnp.int32)
        key_rows = key_tiles[safe_ids].reshape(NB * TILE, HEADS, DH)
        value_rows = value_tiles[safe_ids].reshape(NB * TILE, HEADS, DH)
        key_mask = (listed_live[:, None] & (slot_index[None, :] < tile_counts[safe_ids][:, None])).reshape(NB * TILE)
        return attend_tile(query_tiles[tile_id], key_rows, value_rows, key_mask)

    result = lax.map(one_tile, jnp.arange(NT, dtype=jnp.int32))
    return result.reshape(TOKENS, HEADS * DH)
```

```python
import functools

import jax
import jax.numpy as jnp
from jax import lax
from jax.sharding import PartitionSpec as P
from jax.experimental import pallas as pl
from jax.experimental.pallas import tpu as pltpu

DH = 128
TILE = 384
NB = 8
REACH = 10
HOPS = 4


def shifted(array, axis, by):
    peers = lax.axis_size(axis)
    pairs = [(i, i + by) for i in range(peers) if 0 <= i + by < peers]
    return lax.ppermute(array, axis, pairs)


def attend_kernel(lists_ref, counts_ref, query_ref, *refs):
    key_refs = refs[:NB]
    value_refs = refs[NB : 2 * NB]
    out_ref = refs[2 * NB]
    tile = pl.program_id(0)
    query_rows = query_ref[...]
    slot_index = lax.broadcasted_iota(jnp.int32, (TILE, TILE), 1)
    scores = []
    for entry in range(NB):
        part = lax.dot_general(
            query_rows, key_refs[entry][...], (((1,), (1,)), ((), ())),
            preferred_element_type=jnp.float32,
        ) * DH ** (-0.5)
        live = slot_index < counts_ref[lists_ref[tile, entry]]
        scores.append(jnp.where(live, part, -jnp.inf))
    highest = scores[0].max(axis=1, keepdims=True)
    for part in scores[1:]:
        highest = jnp.maximum(highest, part.max(axis=1, keepdims=True))
    totals = jnp.zeros((TILE, 1), jnp.float32)
    summed = jnp.zeros((TILE, DH), jnp.float32)
    for entry in range(NB):
        weights = jnp.exp(scores[entry] - highest)
        totals = totals + weights.sum(axis=1, keepdims=True)
        summed = summed + jnp.dot(
            weights.astype(jnp.bfloat16), value_refs[entry][...],
            preferred_element_type=jnp.float32,
        )
    out_ref[...] = (summed / totals).astype(out_ref.dtype)


def attend(local_lists, ext_counts, query_tiles, ext_kv):
    tiles_here, _, local_width = query_tiles.shape
    local_heads = local_width // DH
    own = pl.BlockSpec((None, TILE, DH), lambda t, h, lists, counts: (t, 0, h))

    def listed(entry, offset):
        return pl.BlockSpec(
            (None, TILE, DH), lambda t, h, lists, counts: (lists[t, entry], 0, h + offset)
        )

    spec = pltpu.PrefetchScalarGridSpec(
        num_scalar_prefetch=2,
        grid=(tiles_here, local_heads),
        in_specs=[own] + [listed(e, 0) for e in range(NB)] + [listed(e, local_heads) for e in range(NB)],
        out_specs=own,
    )
    return pl.pallas_call(
        attend_kernel,
        grid_spec=spec,
        out_shape=jax.ShapeDtypeStruct(query_tiles.shape, query_tiles.dtype),
        compiler_params=pltpu.CompilerParams(vmem_limit_bytes=48 * 1024 * 1024),
    )(local_lists, ext_counts, query_tiles, *([ext_kv] * (2 * NB)))


MESH = pl.DeviceIdType.MESH
CTX = 4
HEAD = 4
COLS = 3
ROWS = COLS * TILE // HEAD
BLOCK = COLS * TILE
SLOTS = CTX * BLOCK
TILES = CTX * COLS
CHUNK = 96
EXP2_SCALE = DH ** (-0.5) * 1.4426950408889634


def flipped(index, by):
    high = (index // 2 + by // 2) % 2
    low = (index % 2 + by % 2) % 2
    return 2 * high + low


def weighted_mean(query_rows, key_parts, value_parts, bias_parts, out_dtype):
    scores = []
    highest = None
    for key_part, bias in zip(key_parts, bias_parts):
        part = lax.dot_general(
            query_rows, key_part[...], (((1,), (1,)), ((), ())), preferred_element_type=jnp.float32
        ) + bias[...]
        scores.append(part)
        top = part.max(axis=1, keepdims=True)
        highest = top if highest is None else jnp.maximum(highest, top)
    totals = jnp.zeros_like(highest)
    summed = jnp.zeros((query_rows.shape[0], DH), jnp.float32)
    for part, value_part in zip(scores, value_parts):
        weights = jnp.exp2((part - highest) * EXP2_SCALE)
        totals = totals + weights.sum(axis=1, keepdims=True)
        summed = summed + jnp.dot(
            weights.astype(jnp.bfloat16), value_part[...], preferred_element_type=jnp.float32
        )
    return (summed / totals).astype(out_dtype)


def clip_kernel(
    heads, q_hbm, k_hbm, v_hbm, meta_ref, out_hbm,
    kv, qb, ob, metas, bias,
    meta_send, meta_recv, z_send, z_recv, local_sem,
    x_send, x_recv, own_send, own_recv, relay_send, relay_recv, o_send, o_recv,
):
    z = lax.axis_index("ctx")
    r = lax.axis_index("head")
    x_peer = (r + 2) % HEAD
    sibling = flipped(r, 1)
    sources = (k_hbm, v_hbm, q_hbm)

    barrier = pltpu.get_barrier_semaphore()
    for d in range(1, CTX):
        pl.semaphore_signal(barrier, inc=1, device_id={"ctx": flipped(z, d)}, device_id_type=MESH)
    for peer in (x_peer, sibling):
        pl.semaphore_signal(barrier, inc=1, device_id={"head": peer}, device_id_type=MESH)
    pl.semaphore_wait(barrier, CTX + 1)

    def rows_of(block, holder):
        return pl.ds(pl.multiple_of(block * BLOCK + holder * ROWS, ROWS), ROWS)

    def columns_of(owner, head):
        return pl.ds(pl.multiple_of((owner * heads + head) * DH, DH), DH)

    def landing(t, head, block):
        if t < 2:
            return kv.at[head, t, rows_of(block, r)]
        return qb.at[head, block]

    def meta_copy(d):
        return pltpu.make_async_remote_copy(
            meta_ref, metas.at[z], meta_send.at[d], meta_recv.at[d],
            device_id={"ctx": flipped(z, d)}, device_id_type=MESH,
        )

    def z_copy(t, head, d):
        peer = flipped(z, d)
        return pltpu.make_async_remote_copy(
            sources[t].at[:, columns_of(peer, head)], landing(t, head, z),
            z_send.at[t, head, d], z_recv.at[t, head, d],
            device_id={"ctx": peer}, device_id_type=MESH,
        )

    def z_arrival(t, head, d):
        peer = flipped(z, d)
        return pltpu.make_async_remote_copy(
            sources[t].at[:, columns_of(peer, head)], landing(t, head, peer),
            z_send.at[t, head, d], z_recv.at[t, head, d],
            device_id={"ctx": peer}, device_id_type=MESH,
        )

    def local_copy(t, head):
        return pltpu.make_async_copy(
            sources[t].at[:, columns_of(z, head)], landing(t, head, z), local_sem.at[t, head]
        )

    def row_copy(head, d, holder, peer, send, recv):
        piece = kv.at[head, :, rows_of(flipped(z, d), holder)]
        return pltpu.make_async_remote_copy(
            piece, piece, send.at[head, d], recv.at[head, d],
            device_id={"head": peer}, device_id_type=MESH,
        )

    def x_copy(head, d, holder):
        return row_copy(head, d, holder, x_peer, x_send, x_recv)

    def own_copy(head, d, holder):
        return row_copy(head, d, holder, sibling, own_send, own_recv)

    def relay_copy(head, d, holder):
        return row_copy(head, d, holder, sibling, relay_send, relay_recv)

    def out_copy(head, d, owner):
        peer = flipped(z, d)
        return pltpu.make_async_remote_copy(
            ob.at[head, peer], out_hbm.at[:, columns_of(owner, head)],
            o_send.at[head, d], o_recv.at[head, d],
            device_id={"ctx": peer}, device_id_type=MESH,
        )

    def out_local(head):
        return pltpu.make_async_copy(
            ob.at[head, z], out_hbm.at[:, columns_of(z, head)], o_send.at[head, 0]
        )

    for d in (3, 2, 1):
        meta_copy(d).start()
    ORDER = [(0, (0, 1)), (0, (2,)), (1, (0, 1)), (2, (0, 1)), (1, (2,)), (2, (2,))]
    for head, kinds in ORDER:
        for t in kinds:
            for d in (3, 2, 1):
                z_copy(t, head, d).start()
    for head in range(heads):
        for t in range(3):
            local_copy(t, head).start()

    metas[z] = meta_ref[...]
    for d in (1, 2, 3):
        peer = flipped(z, d)
        pltpu.make_async_remote_copy(
            meta_ref, metas.at[peer], meta_send.at[d], meta_recv.at[d],
            device_id={"ctx": peer}, device_id_type=MESH,
        ).wait_recv()
    lane = lax.broadcasted_iota(jnp.int32, (8, 128), 1)
    slot = lax.broadcasted_iota(jnp.int32, (1, TILE), 1)
    for tile in range(TILES):
        where = slice(tile * TILE, (tile + 1) * TILE)
        owner, place = tile // COLS, tile % COLS
        count = metas[owner][place : place + 1, NB : NB + 1]
        live = slot < count
        bias[CTX : CTX + 1, where] = jnp.where(live, 0.0, -jnp.inf)
        for block in range(CTX):
            named = jnp.where((metas[block] == tile) & (lane < NB), 1, 0).max(axis=1, keepdims=True)
            listed = named[1:2, :] > 0
            bias[block : block + 1, where] = jnp.where(live & listed, 0.0, -jnp.inf)

    def forward_own(head):
        for d in range(CTX):
            for t in (0, 1):
                if d == 0:
                    local_copy(t, head).wait()
                else:
                    z_arrival(t, head, d).wait_recv()
            x_copy(head, d, r).start()
            own_copy(head, d, r).start()

    def forward_relay(head):
        for d in range(CTX):
            x_copy(head, d, x_peer).wait_recv()
            relay_copy(head, d, x_peer).start()

    def ready(head):
        for d in range(CTX):
            own_copy(head, d, sibling).wait_recv()
            relay_copy(head, d, flipped(r, 3)).wait_recv()

    is_edge = (r == 0) | (r == HEAD - 1)
    right_side = r // 2
    edge_base = right_side * TILE

    def edge_rows(head, block, start, count):
        parts = [pl.ds(pl.multiple_of(b * BLOCK + edge_base, TILE), 2 * TILE) for b in range(CTX)]
        rows = pl.ds(start, count)
        ob[head, block, rows, :] = weighted_mean(
            qb[head, block, rows, :],
            [kv.at[head, 0, p] for p in parts],
            [kv.at[head, 1, p] for p in parts],
            [bias.at[CTX : CTX + 1, p] for p in parts],
            ob.dtype,
        )

    def center_rows(head, block, start, count):
        parts = [slice(b * BLOCK, (b + 1) * BLOCK) for b in range(CTX)]
        rows = pl.ds(start, count)
        ob[head, block, rows, :] = weighted_mean(
            qb[head, block, rows, :],
            [kv.at[head, 0, p] for p in parts],
            [kv.at[head, 1, p] for p in parts],
            [bias.at[pl.ds(block, 1), p] for p in parts],
            ob.dtype,
        )

    def compute(head):
        def one(d, carry):
            block = flipped(z, d)

            @pl.when(d == 0)
            def _():
                local_copy(2, head).wait()

            @pl.when(d > 0)
            def _():
                z_arrival(2, head, d).wait_recv()

            @pl.when(is_edge)
            def _():
                edge_rows(head, block, 0, ROWS)

            @pl.when(jnp.logical_not(is_edge))
            def _():
                edge_rows(head, block, pl.multiple_of(right_side * 2 * CHUNK, CHUNK), CHUNK)
                center_rows(head, block, pl.multiple_of((1 - right_side) * CHUNK, CHUNK), 2 * CHUNK)

            @pl.when(d == 0)
            def _():
                out_local(head).start()

            @pl.when(d > 0)
            def _():
                out_copy(head, d, z).start()

            return carry

        lax.fori_loop(0, CTX, one, 0)

    forward_own(0)
    forward_relay(0)
    ready(0)
    compute(0)
    forward_own(1)
    forward_relay(1)
    forward_own(2)
    forward_relay(2)
    ready(1)
    compute(1)
    ready(2)
    compute(2)

    for d in (1, 2, 3):
        meta_copy(d).wait_send()
    for head in range(heads):
        for d in range(CTX):
            x_copy(head, d, r).wait_send()
            own_copy(head, d, r).wait_send()
            relay_copy(head, d, x_peer).wait_send()
            if d == 0:
                out_local(head).wait()
            else:
                for t in range(3):
                    z_copy(t, head, d).wait_send()
                out_copy(head, d, z).wait_send()
                out_copy(head, d, flipped(z, d)).wait_recv()


def clip_attention(queries, keys, values, neighbors, tile_counts):
    rows, width = queries.shape
    heads = width // DH // CTX
    meta = jnp.zeros((8, 128), jnp.int32)
    meta = meta.at[:COLS, :NB].set(neighbors).at[:COLS, NB].set(tile_counts)
    anywhere = pl.BlockSpec(memory_space=pl.ANY)
    dma = pltpu.SemaphoreType.DMA
    return pl.pallas_call(
        functools.partial(clip_kernel, heads),
        out_shape=jax.ShapeDtypeStruct((rows, width), queries.dtype),
        in_specs=[anywhere, anywhere, anywhere, pl.BlockSpec(memory_space=pltpu.VMEM)],
        out_specs=anywhere,
        scratch_shapes=[
            pltpu.VMEM((heads, 2, SLOTS, DH), keys.dtype),
            pltpu.VMEM((heads, CTX, ROWS, DH), queries.dtype),
            pltpu.VMEM((heads, CTX, ROWS, DH), queries.dtype),
            pltpu.VMEM((CTX, 8, 128), jnp.int32),
            pltpu.VMEM((8, SLOTS), jnp.float32),
            dma((CTX,)), dma((CTX,)),
            dma((3, heads, CTX)), dma((3, heads, CTX)), dma((3, heads)),
            dma((heads, CTX)), dma((heads, CTX)),
            dma((heads, CTX)), dma((heads, CTX)),
            dma((heads, CTX)), dma((heads, CTX)),
            dma((heads, CTX)), dma((heads, CTX)),
        ],
        compiler_params=pltpu.CompilerParams(
            collective_id=0, has_side_effects=True, vmem_limit_bytes=63 * 1024 * 1024 + 512 * 1024
        ),
    )(queries, keys, values, meta)


def shards(queries, keys, values, neighbors, tile_counts):
    rows, width = queries.shape
    whole_clip = lax.axis_size("ctx") == CTX and lax.axis_size("head") == HEAD
    if whole_clip and tile_counts.shape[0] == COLS:
        return clip_attention(queries, keys, values, neighbors, tile_counts)
    head_peers = lax.axis_size("head")
    group = width // head_peers
    paired = jnp.concatenate(
        [keys.reshape(rows, head_peers, group), values.reshape(rows, head_peers, group)], axis=2
    )
    block_kv = lax.all_to_all(paired, "head", split_axis=1, concat_axis=0, tiled=True)
    block_kv = block_kv.reshape(rows * head_peers, 2 * group)
    tiles_here = tile_counts.shape[0]
    local_heads = group // DH
    ctx_peers = lax.axis_size("ctx")
    if ctx_peers <= 2 * HOPS + 1:
        ext_tiles = ctx_peers * tiles_here
        pieces = jnp.stack([tile_counts // 16, tile_counts % 16], axis=1).astype(jnp.bfloat16)
        ext_kv, pieces = lax.all_gather((block_kv, pieces), "ctx", axis=0, tiled=True)
        pieces = pieces.astype(jnp.int32)
        ext_counts = pieces[:, 0] * 16 + pieces[:, 1]
        first_tile = 0
    else:
        earlier = []
        later = []
        for distance in range(1, HOPS + 1):
            taken = min(tiles_here, REACH - (distance - 1) * tiles_here)
            rows_taken = taken * TILE
            earlier = [shifted((block_kv[-rows_taken:], tile_counts[-taken:]), "ctx", distance)] + earlier
            later = later + [shifted((block_kv[:rows_taken], tile_counts[:taken]), "ctx", -distance)]
        ext_tiles = tiles_here + 2 * REACH
        ext_kv = jnp.concatenate([p[0] for p in earlier] + [block_kv] + [p[0] for p in later], axis=0)
        ext_counts = jnp.concatenate([p[1] for p in earlier] + [tile_counts] + [p[1] for p in later], axis=0)
        first_tile = lax.axis_index("ctx") * tiles_here - REACH
    ext_kv = ext_kv.reshape(ext_tiles, TILE, 2 * group)
    local_lists = jnp.clip(neighbors - first_tile, 0, ext_tiles - 1).astype(jnp.int32)
    block_queries = lax.all_to_all(queries, "head", split_axis=1, concat_axis=0, tiled=True)
    query_tiles = block_queries.reshape(tiles_here, TILE, group)
    outputs = attend(local_lists, ext_counts.astype(jnp.int32), query_tiles, ext_kv)
    outputs = outputs.reshape(tiles_here * TILE, group)
    return lax.all_to_all(outputs, "head", split_axis=0, concat_axis=1, tiled=True)


def solution(mesh):
    placed = (
        P(("clips", "ctx", "head"), None),
        P(("clips", "ctx", "head"), None),
        P(("clips", "ctx", "head"), None),
        P(("clips", "ctx"), None),
        P(("clips", "ctx")),
    )
    return jax.shard_map(
        shards,
        mesh=mesh,
        in_specs=placed,
        out_specs=P(("clips", "ctx", "head"), None),
        check_vma=False,
    )
```

```python
import functools

import jax
import jax.numpy as jnp
from jax import lax
from jax.sharding import PartitionSpec as P
from jax.experimental import pallas as pl
from jax.experimental.pallas import tpu as pltpu

DH = 128
TILE = 384
NB = 8
REACH = 10
HOPS = 4


def shifted(array, axis, by):
    peers = lax.axis_size(axis)
    pairs = [(i, i + by) for i in range(peers) if 0 <= i + by < peers]
    return lax.ppermute(array, axis, pairs)


def attend_kernel(lists_ref, counts_ref, query_ref, *refs):
    key_refs = refs[:NB]
    value_refs = refs[NB : 2 * NB]
    out_ref = refs[2 * NB]
    tile = pl.program_id(0)
    query_rows = query_ref[...]
    slot_index = lax.broadcasted_iota(jnp.int32, (TILE, TILE), 1)
    scores = []
    for entry in range(NB):
        part = lax.dot_general(
            query_rows, key_refs[entry][...], (((1,), (1,)), ((), ())),
            preferred_element_type=jnp.float32,
        ) * DH ** (-0.5)
        live = slot_index < counts_ref[lists_ref[tile, entry]]
        scores.append(jnp.where(live, part, -jnp.inf))
    highest = scores[0].max(axis=1, keepdims=True)
    for part in scores[1:]:
        highest = jnp.maximum(highest, part.max(axis=1, keepdims=True))
    totals = jnp.zeros((TILE, 1), jnp.float32)
    summed = jnp.zeros((TILE, DH), jnp.float32)
    for entry in range(NB):
        weights = jnp.exp(scores[entry] - highest)
        totals = totals + weights.sum(axis=1, keepdims=True)
        summed = summed + jnp.dot(
            weights.astype(jnp.bfloat16), value_refs[entry][...],
            preferred_element_type=jnp.float32,
        )
    out_ref[...] = (summed / totals).astype(out_ref.dtype)


def attend(local_lists, ext_counts, query_tiles, ext_kv):
    tiles_here, _, local_width = query_tiles.shape
    local_heads = local_width // DH
    own = pl.BlockSpec((None, TILE, DH), lambda t, h, lists, counts: (t, 0, h))

    def listed(entry, offset):
        return pl.BlockSpec(
            (None, TILE, DH), lambda t, h, lists, counts: (lists[t, entry], 0, h + offset)
        )

    spec = pltpu.PrefetchScalarGridSpec(
        num_scalar_prefetch=2,
        grid=(tiles_here, local_heads),
        in_specs=[own] + [listed(e, 0) for e in range(NB)] + [listed(e, local_heads) for e in range(NB)],
        out_specs=own,
    )
    return pl.pallas_call(
        attend_kernel,
        grid_spec=spec,
        out_shape=jax.ShapeDtypeStruct(query_tiles.shape, query_tiles.dtype),
        compiler_params=pltpu.CompilerParams(vmem_limit_bytes=48 * 1024 * 1024),
    )(local_lists, ext_counts, query_tiles, *([ext_kv] * (2 * NB)))


MESH = pl.DeviceIdType.MESH
CTX = 4
HEAD = 4
COLS = 3
ROWS = COLS * TILE // HEAD
EDGE = TILE - ROWS
PIECES = ROWS // EDGE
PER_TILE = TILE // EDGE
BLOCK = COLS * TILE
SLOTS = CTX * BLOCK
TILES = CTX * COLS
COUNT_ROW = 8
EXP2_SCALE = DH ** (-0.5) * 1.4426950408889634
FAR_FIRST = (3, 2, 1)
ARRIVAL = (1, 2, 3)


def flipped(index, by):
    high = (index // 2 + by // 2) % 2
    low = (index % 2 + by % 2) % 2
    return 2 * high + low


def attended(query_rows, kv, bias, tiles):
    def rows_of(side, tile):
        return jnp.concatenate([kv[side, tile * PER_TILE + piece] for piece in range(PER_TILE)], axis=0)

    scores = []
    highest = None
    for tile in tiles:
        part = lax.dot_general(
            query_rows, rows_of(0, tile), (((1,), (1,)), ((), ())), preferred_element_type=jnp.float32
        ) + bias[tile]
        scores.append(part)
        top = part.max(axis=1, keepdims=True)
        highest = top if highest is None else jnp.maximum(highest, top)
    totals = jnp.zeros_like(highest)
    summed = jnp.zeros((query_rows.shape[0], DH), jnp.float32)
    for part, tile in zip(scores, tiles):
        weights = jnp.exp2((part - highest) * EXP2_SCALE)
        totals = totals + weights.sum(axis=1, keepdims=True)
        summed = summed + jnp.dot(
            weights.astype(jnp.bfloat16), rows_of(1, tile), preferred_element_type=jnp.float32
        )
    return (summed / totals).astype(query_rows.dtype)


def clip_kernel(
    heads, q_hbm, k_hbm, v_hbm, neighbors_ref, counts_ref, out_hbm, *refs
):
    kvs = refs[:heads]
    (
        qb, ob, meta, metas, bias, lists,
        lists_sem, meta_send, meta_recv, z_send, z_recv, local_sem,
        x_send, x_recv, own_send, own_recv, relay_send, relay_recv,
        o_send, o_recv, e_send, e_recv,
    ) = refs[heads:]
    z = lax.axis_index("ctx")
    r = lax.axis_index("head")
    x_peer = (r + 2) % HEAD
    sibling = flipped(r, 1)
    right = r // 2
    is_side = (r == 0) | (r == HEAD - 1)
    sources = (k_hbm, v_hbm, q_hbm)

    def rows_of(block, holder):
        return pl.ds((block * HEAD + holder) * PIECES, PIECES)

    def columns_of(owner, head):
        return pl.ds(pl.multiple_of((owner * heads + head) * DH, DH), DH)

    def landing(t, head, block):
        if t < 2:
            return kvs[head].at[t, rows_of(block, r)]
        return qb.at[head, block]

    def local_copy(t, head):
        return pltpu.make_async_copy(
            sources[t].at[:, :, columns_of(z, head)], landing(t, head, z), local_sem.at[t, head]
        )

    def meta_copy(d, block):
        return pltpu.make_async_remote_copy(
            meta, metas.at[block], meta_send.at[d], meta_recv.at[d],
            device_id={"ctx": flipped(z, d)}, device_id_type=MESH,
        )

    def z_copy(t, head, d, block):
        peer = flipped(z, d)
        return pltpu.make_async_remote_copy(
            sources[t].at[:, :, columns_of(peer, head)], landing(t, head, block),
            z_send.at[t, head, d], z_recv.at[t, head, d],
            device_id={"ctx": peer}, device_id_type=MESH,
        )

    def row_copy(head, d, holder, peer, send, recv):
        piece = kvs[head].at[:, rows_of(flipped(z, d), holder)]
        return pltpu.make_async_remote_copy(
            piece, piece, send.at[head, d], recv.at[head, d],
            device_id={"head": peer}, device_id_type=MESH,
        )

    def x_copy(head, d, holder):
        return row_copy(head, d, holder, x_peer, x_send, x_recv)

    def own_copy(head, d, holder):
        return row_copy(head, d, holder, sibling, own_send, own_recv)

    def relay_copy(head, d, holder):
        return row_copy(head, d, holder, sibling, relay_send, relay_recv)

    side_rows = (0, ROWS)
    middle_rows = (pl.multiple_of((1 - right) * EDGE, EDGE), ROWS - EDGE)
    edge_rows = (pl.multiple_of(right * (ROWS - EDGE), EDGE), EDGE)

    def out_copy(head, d, owner, rows, send, recv):
        peer = flipped(z, d)
        where = pl.ds(*rows)
        return pltpu.make_async_remote_copy(
            ob.at[head, peer, where], out_hbm.at[where, columns_of(owner, head)],
            send.at[head, d], recv.at[head, d],
            device_id={"ctx": peer}, device_id_type=MESH,
        )

    def out_local(head, rows, send):
        where = pl.ds(*rows)
        return pltpu.make_async_copy(
            ob.at[head, z, where], out_hbm.at[where, columns_of(z, head)], send.at[head, 0]
        )

    for head in range(heads):
        for t in range(3):
            local_copy(t, head).start()
    meta[:COLS, :NB] = neighbors_ref[...]
    for place in range(COLS):
        row = COUNT_ROW + place
        meta[row : row + 1, :] = jnp.full((1, 128), counts_ref[place], jnp.int32)

    barrier = pltpu.get_barrier_semaphore()
    for d in range(1, CTX):
        pl.semaphore_signal(barrier, inc=1, device_id={"ctx": flipped(z, d)}, device_id_type=MESH)
    for peer in (x_peer, sibling):
        pl.semaphore_signal(barrier, inc=1, device_id={"head": peer}, device_id_type=MESH)
    pl.semaphore_wait(barrier, CTX + 1)

    for d in FAR_FIRST:
        meta_copy(d, z).start()
    for head, kinds in ((0, (0, 1)), (0, (2,)), (1, (0, 1)), (2, (0, 1)), (1, (2,)), (2, (2,))):
        for t in kinds:
            for d in FAR_FIRST:
                z_copy(t, head, d, z).start()
    for head in range(heads):
        local_copy(0, head).wait()
        local_copy(1, head).wait()
        x_copy(head, 0, r).start()
        own_copy(head, 0, r).start()

    metas[z] = meta[...]
    for d in ARRIVAL:
        meta_copy(d, flipped(z, d)).wait_recv()
    to_scalars = pltpu.make_async_copy(metas, lists, lists_sem)
    to_scalars.start()
    slot = lax.broadcasted_iota(jnp.int32, (1, TILE), 1)
    for tile in range(TILES):
        row = COUNT_ROW + tile % COLS
        count = metas[tile // COLS, row : row + 1, :1]
        bias[tile] = jnp.where(slot < count, 0.0, -jnp.inf)
    to_scalars.wait()

    def forward_own(head):
        for d in ARRIVAL:
            for t in (0, 1):
                z_copy(t, head, d, flipped(z, d)).wait_recv()
            x_copy(head, d, r).start()
            own_copy(head, d, r).start()

    def forward_relay(head):
        for d in (0,) + ARRIVAL:
            x_copy(head, d, x_peer).wait_recv()
            relay_copy(head, d, x_peer).start()

    def ready(head):
        for d in (0,) + ARRIVAL:
            own_copy(head, d, sibling).wait_recv()
            relay_copy(head, d, flipped(r, 3)).wait_recv()

    side_tiles = [b * COLS + right + side for b in range(CTX) for side in range(2)]

    def await_queries(head, d):
        @pl.when(d == 0)
        def _():
            local_copy(2, head).wait()

        @pl.when(d > 0)
        def _():
            z_copy(2, head, d, flipped(z, d)).wait_recv()

    def send_out(head, d, rows, send, recv):
        @pl.when(d == 0)
        def _():
            out_local(head, rows, send).start()

        @pl.when(d > 0)
        def _():
            out_copy(head, d, z, rows, send, recv).start()

    def compute(head):
        def one(step, carry):
            d = (step + 1) % CTX
            block = flipped(z, d)
            await_queries(head, d)

            @pl.when(is_side)
            def _():
                rows = pl.ds(*side_rows)
                queries = jnp.concatenate([qb[head, block, piece] for piece in range(PIECES)], axis=0)
                ob[head, block, rows, :] = attended(queries, kvs[head], bias, side_tiles)
                send_out(head, d, side_rows, o_send, o_recv)

            @pl.when(jnp.logical_not(is_side))
            def _():
                rows = pl.ds(*middle_rows)
                tiles = [lists[block, 1, entry] for entry in range(NB)]
                queries = jnp.concatenate([qb[head, block, 1 - right + piece] for piece in range(2)], axis=0)
                ob[head, block, rows, :] = attended(queries, kvs[head], bias, tiles)
                send_out(head, d, middle_rows, o_send, o_recv)

            return carry

        lax.fori_loop(0, CTX, one, 0)

        @pl.when(jnp.logical_not(is_side))
        def _():
            rows = pl.ds(*edge_rows)
            gathered = jnp.concatenate([qb[head, block, 2 * right] for block in range(CTX)], axis=0)
            result = attended(gathered, kvs[head], bias, side_tiles)
            for block in range(CTX):
                ob[head, block, rows, :] = result[block * EDGE : (block + 1) * EDGE]
            for d in FAR_FIRST:
                out_copy(head, d, z, edge_rows, e_send, e_recv).start()
            out_local(head, edge_rows, e_send).start()

    forward_own(0)
    forward_relay(0)
    ready(0)
    compute(0)
    forward_own(1)
    forward_relay(1)
    forward_own(2)
    forward_relay(2)
    ready(1)
    compute(1)
    ready(2)
    compute(2)

    def settle(head, rows, send, recv):
        out_local(head, rows, send).wait()
        for d in ARRIVAL:
            out_copy(head, d, z, rows, send, recv).wait_send()
            out_copy(head, d, flipped(z, d), rows, send, recv).wait_recv()

    for d in ARRIVAL:
        meta_copy(d, z).wait_send()
    for head in range(heads):
        for d in range(CTX):
            x_copy(head, d, r).wait_send()
            own_copy(head, d, r).wait_send()
            relay_copy(head, d, x_peer).wait_send()
        for d in ARRIVAL:
            for t in range(3):
                z_copy(t, head, d, z).wait_send()

    @pl.when(is_side)
    def _():
        for head in range(heads):
            settle(head, side_rows, o_send, o_recv)

    @pl.when(jnp.logical_not(is_side))
    def _():
        for head in range(heads):
            settle(head, middle_rows, o_send, o_recv)
            settle(head, edge_rows, e_send, e_recv)


def clip_attention(queries, keys, values, neighbors, tile_counts):
    rows, width = queries.shape
    heads = width // DH // CTX
    anywhere = pl.BlockSpec(memory_space=pl.ANY)
    dma = pltpu.SemaphoreType.DMA
    each = dma((heads, CTX))
    queries, keys, values = (
        array.reshape(PIECES, EDGE, width) for array in (queries, keys, values)
    )
    return pl.pallas_call(
        functools.partial(clip_kernel, heads),
        out_shape=jax.ShapeDtypeStruct((rows, width), queries.dtype),
        in_specs=[anywhere] * 3 + [
            pl.BlockSpec(memory_space=pltpu.VMEM), pl.BlockSpec(memory_space=pltpu.SMEM)
        ],
        out_specs=anywhere,
        scratch_shapes=[pltpu.VMEM((2, TILES * PER_TILE, EDGE, DH), keys.dtype)] * heads + [
            pltpu.VMEM((heads, CTX, PIECES, EDGE, DH), queries.dtype),
            pltpu.VMEM((heads, CTX, ROWS, DH), queries.dtype),
            pltpu.VMEM((16, 128), jnp.int32),
            pltpu.VMEM((CTX, 16, 128), jnp.int32),
            pltpu.VMEM((TILES, 1, TILE), jnp.float32),
            pltpu.SMEM((CTX, 16, 128), jnp.int32),
            dma, dma((CTX,)), dma((CTX,)),
            dma((3, heads, CTX)), dma((3, heads, CTX)), dma((3, heads)),
        ] + [each] * 10,
        compiler_params=pltpu.CompilerParams(
            collective_id=0, has_side_effects=True, vmem_limit_bytes=63 * 1024 * 1024 + 512 * 1024
        ),
    )(queries, keys, values, neighbors, tile_counts)


def shards(queries, keys, values, neighbors, tile_counts):
    rows, width = queries.shape
    whole_clip = lax.axis_size("ctx") == CTX and lax.axis_size("head") == HEAD
    if whole_clip and tile_counts.shape[0] == COLS:
        return clip_attention(queries, keys, values, neighbors, tile_counts)
    head_peers = lax.axis_size("head")
    group = width // head_peers
    paired = jnp.concatenate(
        [keys.reshape(rows, head_peers, group), values.reshape(rows, head_peers, group)], axis=2
    )
    block_kv = lax.all_to_all(paired, "head", split_axis=1, concat_axis=0, tiled=True)
    block_kv = block_kv.reshape(rows * head_peers, 2 * group)
    tiles_here = tile_counts.shape[0]
    local_heads = group // DH
    ctx_peers = lax.axis_size("ctx")
    if ctx_peers <= 2 * HOPS + 1:
        ext_tiles = ctx_peers * tiles_here
        pieces = jnp.stack([tile_counts // 16, tile_counts % 16], axis=1).astype(jnp.bfloat16)
        ext_kv, pieces = lax.all_gather((block_kv, pieces), "ctx", axis=0, tiled=True)
        pieces = pieces.astype(jnp.int32)
        ext_counts = pieces[:, 0] * 16 + pieces[:, 1]
        first_tile = 0
    else:
        earlier = []
        later = []
        for distance in range(1, HOPS + 1):
            taken = min(tiles_here, REACH - (distance - 1) * tiles_here)
            rows_taken = taken * TILE
            earlier = [shifted((block_kv[-rows_taken:], tile_counts[-taken:]), "ctx", distance)] + earlier
            later = later + [shifted((block_kv[:rows_taken], tile_counts[:taken]), "ctx", -distance)]
        ext_tiles = tiles_here + 2 * REACH
        ext_kv = jnp.concatenate([p[0] for p in earlier] + [block_kv] + [p[0] for p in later], axis=0)
        ext_counts = jnp.concatenate([p[1] for p in earlier] + [tile_counts] + [p[1] for p in later], axis=0)
        first_tile = lax.axis_index("ctx") * tiles_here - REACH
    ext_kv = ext_kv.reshape(ext_tiles, TILE, 2 * group)
    local_lists = jnp.clip(neighbors - first_tile, 0, ext_tiles - 1).astype(jnp.int32)
    block_queries = lax.all_to_all(queries, "head", split_axis=1, concat_axis=0, tiled=True)
    query_tiles = block_queries.reshape(tiles_here, TILE, group)
    outputs = attend(local_lists, ext_counts.astype(jnp.int32), query_tiles, ext_kv)
    outputs = outputs.reshape(tiles_here * TILE, group)
    return lax.all_to_all(outputs, "head", split_axis=0, concat_axis=1, tiled=True)


def solution(mesh):
    placed = (
        P(("clips", "ctx", "head"), None),
        P(("clips", "ctx", "head"), None),
        P(("clips", "ctx", "head"), None),
        P(("clips", "ctx"), None),
        P(("clips", "ctx")),
    )
    return jax.shard_map(
        shards,
        mesh=mesh,
        in_specs=placed,
        out_specs=P(("clips", "ctx", "head"), None),
        check_vma=False,
    )
```

```python
import functools

import jax
import jax.numpy as jnp
from jax import lax
from jax.sharding import PartitionSpec as P
from jax.experimental import pallas as pl
from jax.experimental.pallas import tpu as pltpu

DH = 128
TILE = 384
NB = 8
REACH = 10
HOPS = 4


def shifted(array, axis, by):
    peers = lax.axis_size(axis)
    pairs = [(i, i + by) for i in range(peers) if 0 <= i + by < peers]
    return lax.ppermute(array, axis, pairs)


def attend_kernel(lists_ref, counts_ref, query_ref, *refs):
    key_refs = refs[:NB]
    value_refs = refs[NB : 2 * NB]
    out_ref = refs[2 * NB]
    tile = pl.program_id(0)
    query_rows = query_ref[...]
    slot_index = lax.broadcasted_iota(jnp.int32, (TILE, TILE), 1)
    scores = []
    for entry in range(NB):
        part = lax.dot_general(
            query_rows, key_refs[entry][...], (((1,), (1,)), ((), ())),
            preferred_element_type=jnp.float32,
        ) * DH ** (-0.5)
        live = slot_index < counts_ref[lists_ref[tile, entry]]
        scores.append(jnp.where(live, part, -jnp.inf))
    highest = scores[0].max(axis=1, keepdims=True)
    for part in scores[1:]:
        highest = jnp.maximum(highest, part.max(axis=1, keepdims=True))
    totals = jnp.zeros((TILE, 1), jnp.float32)
    summed = jnp.zeros((TILE, DH), jnp.float32)
    for entry in range(NB):
        weights = jnp.exp(scores[entry] - highest)
        totals = totals + weights.sum(axis=1, keepdims=True)
        summed = summed + jnp.dot(
            weights.astype(jnp.bfloat16), value_refs[entry][...],
            preferred_element_type=jnp.float32,
        )
    out_ref[...] = (summed / totals).astype(out_ref.dtype)


def attend(local_lists, ext_counts, query_tiles, ext_kv):
    tiles_here, _, local_width = query_tiles.shape
    local_heads = local_width // DH
    own = pl.BlockSpec((None, TILE, DH), lambda t, h, lists, counts: (t, 0, h))

    def listed(entry, offset):
        return pl.BlockSpec(
            (None, TILE, DH), lambda t, h, lists, counts: (lists[t, entry], 0, h + offset)
        )

    spec = pltpu.PrefetchScalarGridSpec(
        num_scalar_prefetch=2,
        grid=(tiles_here, local_heads),
        in_specs=[own] + [listed(e, 0) for e in range(NB)] + [listed(e, local_heads) for e in range(NB)],
        out_specs=own,
    )
    return pl.pallas_call(
        attend_kernel,
        grid_spec=spec,
        out_shape=jax.ShapeDtypeStruct(query_tiles.shape, query_tiles.dtype),
        compiler_params=pltpu.CompilerParams(vmem_limit_bytes=48 * 1024 * 1024),
    )(local_lists, ext_counts, query_tiles, *([ext_kv] * (2 * NB)))


MESH = pl.DeviceIdType.MESH
CTX = 4
HEAD = 4
COLS = 3
ROWS = COLS * TILE // HEAD
EDGE = TILE - ROWS
PIECES = ROWS // EDGE
PER_TILE = TILE // EDGE
BLOCK = COLS * TILE
SLOTS = CTX * BLOCK
TILES = CTX * COLS
COUNT_ROW = 8
EXP2_SCALE = DH ** (-0.5) * 1.4426950408889634
FAR_FIRST = (2, 3, 1)
ARRIVAL = (1, 2, 3)


def flipped(index, by):
    high = (index // 2 + by // 2) % 2
    low = (index % 2 + by % 2) % 2
    return 2 * high + low


def attended(query_rows, kv, bias, tiles):
    def rows_of(side, tile):
        return jnp.concatenate([kv[side, tile * PER_TILE + piece] for piece in range(PER_TILE)], axis=0)

    scores = []
    highest = None
    for tile in tiles:
        part = lax.dot_general(
            query_rows, rows_of(0, tile), (((1,), (1,)), ((), ())), preferred_element_type=jnp.float32
        ) + bias[tile]
        scores.append(part)
        top = part.max(axis=1, keepdims=True)
        highest = top if highest is None else jnp.maximum(highest, top)
    totals = jnp.zeros_like(highest)
    summed = jnp.zeros((query_rows.shape[0], DH), jnp.float32)
    for part, tile in zip(scores, tiles):
        weights = jnp.exp2((part - highest) * EXP2_SCALE)
        totals = totals + weights.sum(axis=1, keepdims=True)
        summed = summed + jnp.dot(
            weights.astype(jnp.bfloat16), rows_of(1, tile), preferred_element_type=jnp.float32
        )
    return (summed / totals).astype(query_rows.dtype)


def clip_kernel(
    heads, q_hbm, k_hbm, v_hbm, neighbors_ref, counts_ref, out_hbm, *refs
):
    kvs = refs[:heads]
    (
        qb, ob, meta, metas, bias, lists,
        lists_sem, meta_send, meta_recv, z_send, z_recv, local_sem,
        x_send, x_recv, own_send, own_recv, relay_send, relay_recv,
        o_send, o_recv, e_send, e_recv,
    ) = refs[heads:]
    z = lax.axis_index("ctx")
    r = lax.axis_index("head")
    x_peer = (r + 2) % HEAD
    sibling = flipped(r, 1)
    right = r // 2
    is_side = (r == 0) | (r == HEAD - 1)
    sources = (k_hbm, v_hbm, q_hbm)

    def rows_of(block, holder):
        return pl.ds((block * HEAD + holder) * PIECES, PIECES)

    def columns_of(owner, head):
        return pl.ds(pl.multiple_of((owner * heads + head) * DH, DH), DH)

    def landing(t, head, block):
        if t < 2:
            return kvs[head].at[t, rows_of(block, r)]
        return qb.at[head, block]

    def local_copy(t, head):
        return pltpu.make_async_copy(
            sources[t].at[:, :, columns_of(z, head)], landing(t, head, z), local_sem.at[t, head]
        )

    def meta_copy(d, block):
        return pltpu.make_async_remote_copy(
            meta, metas.at[block], meta_send.at[d], meta_recv.at[d],
            device_id={"ctx": flipped(z, d)}, device_id_type=MESH,
        )

    def z_copy(t, head, d, block):
        peer = flipped(z, d)
        return pltpu.make_async_remote_copy(
            sources[t].at[:, :, columns_of(peer, head)], landing(t, head, block),
            z_send.at[t, head, d], z_recv.at[t, head, d],
            device_id={"ctx": peer}, device_id_type=MESH,
        )

    def row_copy(head, d, holder, peer, send, recv):
        piece = kvs[head].at[:, rows_of(flipped(z, d), holder)]
        return pltpu.make_async_remote_copy(
            piece, piece, send.at[head, d], recv.at[head, d],
            device_id={"head": peer}, device_id_type=MESH,
        )

    def x_copy(head, d, holder):
        return row_copy(head, d, holder, x_peer, x_send, x_recv)

    def own_copy(head, d, holder):
        return row_copy(head, d, holder, sibling, own_send, own_recv)

    def relay_copy(head, d, holder):
        return row_copy(head, d, holder, sibling, relay_send, relay_recv)

    side_rows = (0, ROWS)
    middle_rows = (pl.multiple_of((1 - right) * EDGE, EDGE), ROWS - EDGE)
    edge_rows = (pl.multiple_of(right * (ROWS - EDGE), EDGE), EDGE)

    def out_copy(head, d, owner, rows, send, recv):
        peer = flipped(z, d)
        where = pl.ds(*rows)
        return pltpu.make_async_remote_copy(
            ob.at[head, peer, where], out_hbm.at[where, columns_of(owner, head)],
            send.at[head, d], recv.at[head, d],
            device_id={"ctx": peer}, device_id_type=MESH,
        )

    def out_local(head, rows, send):
        where = pl.ds(*rows)
        return pltpu.make_async_copy(
            ob.at[head, z, where], out_hbm.at[where, columns_of(z, head)], send.at[head, 0]
        )

    for head in range(heads):
        for t in range(3):
            local_copy(t, head).start()
    meta[:COLS, :NB] = neighbors_ref[...]
    for place in range(COLS):
        row = COUNT_ROW + place
        meta[row : row + 1, :] = jnp.full((1, 128), counts_ref[place], jnp.int32)

    barrier = pltpu.get_barrier_semaphore()
    for d in range(1, CTX):
        pl.semaphore_signal(barrier, inc=1, device_id={"ctx": flipped(z, d)}, device_id_type=MESH)
    for peer in (x_peer, sibling):
        pl.semaphore_signal(barrier, inc=1, device_id={"head": peer}, device_id_type=MESH)
    pl.semaphore_wait(barrier, CTX + 1)

    for d in FAR_FIRST:
        meta_copy(d, z).start()
    def send_kv(head):
        for t in (0, 1):
            for d in FAR_FIRST:
                z_copy(t, head, d, z).start()

    def send_q(head):
        for d in FAR_FIRST:
            z_copy(2, head, d, z).start()

    send_kv(0)
    send_kv(1)
    send_q(0)
    send_kv(2)
    send_q(1)
    send_q(2)
    for head in range(heads):
        local_copy(0, head).wait()
        local_copy(1, head).wait()
        x_copy(head, 0, r).start()
        own_copy(head, 0, r).start()

    metas[z] = meta[...]
    for d in ARRIVAL:
        meta_copy(d, flipped(z, d)).wait_recv()
    to_scalars = pltpu.make_async_copy(metas, lists, lists_sem)
    to_scalars.start()
    slot = lax.broadcasted_iota(jnp.int32, (1, TILE), 1)
    for tile in range(TILES):
        row = COUNT_ROW + tile % COLS
        count = metas[tile // COLS, row : row + 1, :1]
        bias[tile] = jnp.where(slot < count, 0.0, -jnp.inf)
    to_scalars.wait()

    def forward_own(head):
        for d in ARRIVAL:
            for t in (0, 1):
                z_copy(t, head, d, flipped(z, d)).wait_recv()
            x_copy(head, d, r).start()
            own_copy(head, d, r).start()

    def forward_relay(head):
        for d in (0,) + ARRIVAL:
            x_copy(head, d, x_peer).wait_recv()
            relay_copy(head, d, x_peer).start()

    def ready(head):
        for d in (0,) + ARRIVAL:
            own_copy(head, d, sibling).wait_recv()
            relay_copy(head, d, flipped(r, 3)).wait_recv()

    side_tiles = [b * COLS + right + side for b in range(CTX) for side in range(2)]

    def await_queries(head, d):
        @pl.when(d == 0)
        def _():
            local_copy(2, head).wait()

        @pl.when(d > 0)
        def _():
            z_copy(2, head, d, flipped(z, d)).wait_recv()

    def send_out(head, d, rows, send, recv):
        @pl.when(d == 0)
        def _():
            out_local(head, rows, send).start()

        @pl.when(d > 0)
        def _():
            out_copy(head, d, z, rows, send, recv).start()

    def compute(head):
        def one(step, carry):
            d = (step + 2) % CTX
            block = flipped(z, d)
            await_queries(head, d)

            @pl.when(is_side)
            def _():
                rows = pl.ds(*side_rows)
                queries = jnp.concatenate([qb[head, block, piece] for piece in range(PIECES)], axis=0)
                ob[head, block, rows, :] = attended(queries, kvs[head], bias, side_tiles)
                send_out(head, d, side_rows, o_send, o_recv)

            @pl.when(jnp.logical_not(is_side))
            def _():
                rows = pl.ds(*middle_rows)
                tiles = [lists[block, 1, entry] for entry in range(NB)]
                queries = jnp.concatenate([qb[head, block, 1 - right + piece] for piece in range(2)], axis=0)
                ob[head, block, rows, :] = attended(queries, kvs[head], bias, tiles)
                send_out(head, d, middle_rows, o_send, o_recv)

            return carry

        lax.fori_loop(0, CTX, one, 0)

        @pl.when(jnp.logical_not(is_side))
        def _():
            rows = pl.ds(*edge_rows)
            gathered = jnp.concatenate([qb[head, block, 2 * right] for block in range(CTX)], axis=0)
            result = attended(gathered, kvs[head], bias, side_tiles)
            for block in range(CTX):
                ob[head, block, rows, :] = result[block * EDGE : (block + 1) * EDGE]
            for d in FAR_FIRST:
                out_copy(head, d, z, edge_rows, e_send, e_recv).start()
            out_local(head, edge_rows, e_send).start()

    forward_own(0)
    forward_relay(0)
    forward_own(1)
    ready(0)
    compute(0)
    forward_relay(1)
    forward_own(2)
    ready(1)
    compute(1)
    forward_relay(2)
    ready(2)
    compute(2)

    def settle(head, rows, send, recv):
        out_local(head, rows, send).wait()
        for d in ARRIVAL:
            out_copy(head, d, z, rows, send, recv).wait_send()
            out_copy(head, d, flipped(z, d), rows, send, recv).wait_recv()

    for d in ARRIVAL:
        meta_copy(d, z).wait_send()
    for head in range(heads):
        for d in range(CTX):
            x_copy(head, d, r).wait_send()
            own_copy(head, d, r).wait_send()
            relay_copy(head, d, x_peer).wait_send()
        for d in ARRIVAL:
            for t in range(3):
                z_copy(t, head, d, z).wait_send()

    @pl.when(is_side)
    def _():
        for head in range(heads):
            settle(head, side_rows, o_send, o_recv)

    @pl.when(jnp.logical_not(is_side))
    def _():
        for head in range(heads):
            settle(head, middle_rows, o_send, o_recv)
            settle(head, edge_rows, e_send, e_recv)


def clip_attention(queries, keys, values, neighbors, tile_counts):
    rows, width = queries.shape
    heads = width // DH // CTX
    anywhere = pl.BlockSpec(memory_space=pl.ANY)
    dma = pltpu.SemaphoreType.DMA
    each = dma((heads, CTX))
    queries, keys, values = (
        array.reshape(PIECES, EDGE, width) for array in (queries, keys, values)
    )
    return pl.pallas_call(
        functools.partial(clip_kernel, heads),
        out_shape=jax.ShapeDtypeStruct((rows, width), queries.dtype),
        in_specs=[anywhere] * 3 + [
            pl.BlockSpec(memory_space=pltpu.VMEM), pl.BlockSpec(memory_space=pltpu.SMEM)
        ],
        out_specs=anywhere,
        scratch_shapes=[pltpu.VMEM((2, TILES * PER_TILE, EDGE, DH), keys.dtype)] * heads + [
            pltpu.VMEM((heads, CTX, PIECES, EDGE, DH), queries.dtype),
            pltpu.VMEM((heads, CTX, ROWS, DH), queries.dtype),
            pltpu.VMEM((16, 128), jnp.int32),
            pltpu.VMEM((CTX, 16, 128), jnp.int32),
            pltpu.VMEM((TILES, 1, TILE), jnp.float32),
            pltpu.SMEM((CTX, 16, 128), jnp.int32),
            dma, dma((CTX,)), dma((CTX,)),
            dma((3, heads, CTX)), dma((3, heads, CTX)), dma((3, heads)),
        ] + [each] * 10,
        compiler_params=pltpu.CompilerParams(
            collective_id=0, has_side_effects=True, vmem_limit_bytes=63 * 1024 * 1024 + 512 * 1024
        ),
    )(queries, keys, values, neighbors, tile_counts)


def shards(queries, keys, values, neighbors, tile_counts):
    rows, width = queries.shape
    whole_clip = lax.axis_size("ctx") == CTX and lax.axis_size("head") == HEAD
    if whole_clip and tile_counts.shape[0] == COLS:
        return clip_attention(queries, keys, values, neighbors, tile_counts)
    head_peers = lax.axis_size("head")
    group = width // head_peers
    paired = jnp.concatenate(
        [keys.reshape(rows, head_peers, group), values.reshape(rows, head_peers, group)], axis=2
    )
    block_kv = lax.all_to_all(paired, "head", split_axis=1, concat_axis=0, tiled=True)
    block_kv = block_kv.reshape(rows * head_peers, 2 * group)
    tiles_here = tile_counts.shape[0]
    local_heads = group // DH
    ctx_peers = lax.axis_size("ctx")
    if ctx_peers <= 2 * HOPS + 1:
        ext_tiles = ctx_peers * tiles_here
        pieces = jnp.stack([tile_counts // 16, tile_counts % 16], axis=1).astype(jnp.bfloat16)
        ext_kv, pieces = lax.all_gather((block_kv, pieces), "ctx", axis=0, tiled=True)
        pieces = pieces.astype(jnp.int32)
        ext_counts = pieces[:, 0] * 16 + pieces[:, 1]
        first_tile = 0
    else:
        earlier = []
        later = []
        for distance in range(1, HOPS + 1):
            taken = min(tiles_here, REACH - (distance - 1) * tiles_here)
            rows_taken = taken * TILE
            earlier = [shifted((block_kv[-rows_taken:], tile_counts[-taken:]), "ctx", distance)] + earlier
            later = later + [shifted((block_kv[:rows_taken], tile_counts[:taken]), "ctx", -distance)]
        ext_tiles = tiles_here + 2 * REACH
        ext_kv = jnp.concatenate([p[0] for p in earlier] + [block_kv] + [p[0] for p in later], axis=0)
        ext_counts = jnp.concatenate([p[1] for p in earlier] + [tile_counts] + [p[1] for p in later], axis=0)
        first_tile = lax.axis_index("ctx") * tiles_here - REACH
    ext_kv = ext_kv.reshape(ext_tiles, TILE, 2 * group)
    local_lists = jnp.clip(neighbors - first_tile, 0, ext_tiles - 1).astype(jnp.int32)
    block_queries = lax.all_to_all(queries, "head", split_axis=1, concat_axis=0, tiled=True)
    query_tiles = block_queries.reshape(tiles_here, TILE, group)
    outputs = attend(local_lists, ext_counts.astype(jnp.int32), query_tiles, ext_kv)
    outputs = outputs.reshape(tiles_here * TILE, group)
    return lax.all_to_all(outputs, "head", split_axis=0, concat_axis=1, tiled=True)


def solution(mesh):
    placed = (
        P(("clips", "ctx", "head"), None),
        P(("clips", "ctx", "head"), None),
        P(("clips", "ctx", "head"), None),
        P(("clips", "ctx"), None),
        P(("clips", "ctx")),
    )
    return jax.shard_map(
        shards,
        mesh=mesh,
        in_specs=placed,
        out_specs=P(("clips", "ctx", "head"), None),
        check_vma=False,
    )
```

```python
import functools

import jax
import jax.numpy as jnp
from jax import lax
from jax.sharding import PartitionSpec as P
from jax.experimental import pallas as pl
from jax.experimental.pallas import tpu as pltpu

DH = 128
TILE = 384
NB = 8
REACH = 10
HOPS = 4


def shifted(array, axis, by):
    peers = lax.axis_size(axis)
    pairs = [(i, i + by) for i in range(peers) if 0 <= i + by < peers]
    return lax.ppermute(array, axis, pairs)


def attend_kernel(lists_ref, counts_ref, query_ref, *refs):
    key_refs = refs[:NB]
    value_refs = refs[NB : 2 * NB]
    out_ref = refs[2 * NB]
    tile = pl.program_id(0)
    query_rows = query_ref[...]
    slot_index = lax.broadcasted_iota(jnp.int32, (TILE, TILE), 1)
    scores = []
    for entry in range(NB):
        part = lax.dot_general(
            query_rows, key_refs[entry][...], (((1,), (1,)), ((), ())),
            preferred_element_type=jnp.float32,
        ) * DH ** (-0.5)
        live = slot_index < counts_ref[lists_ref[tile, entry]]
        scores.append(jnp.where(live, part, -jnp.inf))
    highest = scores[0].max(axis=1, keepdims=True)
    for part in scores[1:]:
        highest = jnp.maximum(highest, part.max(axis=1, keepdims=True))
    totals = jnp.zeros((TILE, 1), jnp.float32)
    summed = jnp.zeros((TILE, DH), jnp.float32)
    for entry in range(NB):
        weights = jnp.exp(scores[entry] - highest)
        totals = totals + weights.sum(axis=1, keepdims=True)
        summed = summed + jnp.dot(
            weights.astype(jnp.bfloat16), value_refs[entry][...],
            preferred_element_type=jnp.float32,
        )
    out_ref[...] = (summed / totals).astype(out_ref.dtype)


def attend(local_lists, ext_counts, query_tiles, ext_kv):
    tiles_here, _, local_width = query_tiles.shape
    local_heads = local_width // DH
    own = pl.BlockSpec((None, TILE, DH), lambda t, h, lists, counts: (t, 0, h))

    def listed(entry, offset):
        return pl.BlockSpec(
            (None, TILE, DH), lambda t, h, lists, counts: (lists[t, entry], 0, h + offset)
        )

    spec = pltpu.PrefetchScalarGridSpec(
        num_scalar_prefetch=2,
        grid=(tiles_here, local_heads),
        in_specs=[own] + [listed(e, 0) for e in range(NB)] + [listed(e, local_heads) for e in range(NB)],
        out_specs=own,
    )
    return pl.pallas_call(
        attend_kernel,
        grid_spec=spec,
        out_shape=jax.ShapeDtypeStruct(query_tiles.shape, query_tiles.dtype),
        compiler_params=pltpu.CompilerParams(vmem_limit_bytes=48 * 1024 * 1024),
    )(local_lists, ext_counts, query_tiles, *([ext_kv] * (2 * NB)))


MESH = pl.DeviceIdType.MESH
CTX = 4
HEAD = 4
COLS = 3
ROWS = COLS * TILE // HEAD
EDGE = TILE - ROWS
PIECES = ROWS // EDGE
PER_TILE = TILE // EDGE
BLOCK = COLS * TILE
SLOTS = CTX * BLOCK
TILES = CTX * COLS
COUNT_ROW = 8
EXP2_SCALE = DH ** (-0.5) * 1.4426950408889634
FAR_FIRST = (2, 3, 1)
ARRIVAL = (1, 2, 3)


def flipped(index, by):
    high = (index // 2 + by // 2) % 2
    low = (index % 2 + by % 2) % 2
    return 2 * high + low


def attended(query_rows, kv, bias, tiles):
    def rows_of(side, tile):
        return jnp.concatenate([kv[side, tile * PER_TILE + piece] for piece in range(PER_TILE)], axis=0)

    scores = []
    highest = None
    for tile in tiles:
        part = lax.dot_general(
            query_rows, rows_of(0, tile), (((1,), (1,)), ((), ())), preferred_element_type=jnp.float32
        ) + bias[tile]
        scores.append(part)
        top = part.max(axis=1, keepdims=True)
        highest = top if highest is None else jnp.maximum(highest, top)
    totals = jnp.zeros_like(highest)
    summed = jnp.zeros((query_rows.shape[0], DH), jnp.float32)
    for part, tile in zip(scores, tiles):
        weights = jnp.exp2((part - highest) * EXP2_SCALE)
        totals = totals + weights.sum(axis=1, keepdims=True)
        summed = summed + jnp.dot(
            weights.astype(jnp.bfloat16), rows_of(1, tile), preferred_element_type=jnp.float32
        )
    return (summed / totals).astype(query_rows.dtype)


def clip_kernel(
    heads, q_hbm, k_hbm, v_hbm, neighbors_ref, counts_ref, out_ref, *refs
):
    kvs = refs[:heads]
    (
        qb, ob, meta, metas, bias, lists,
        lists_sem, meta_send, meta_recv, z_send, z_recv, local_sem,
        x_send, x_recv, own_send, own_recv, relay_send, relay_recv,
        o_send, o_recv, e_send, e_recv,
    ) = refs[heads:]
    z = lax.axis_index("ctx")
    r = lax.axis_index("head")
    x_peer = (r + 2) % HEAD
    sibling = flipped(r, 1)
    right = r // 2
    is_side = (r == 0) | (r == HEAD - 1)
    sources = (k_hbm, v_hbm, q_hbm)

    def rows_of(block, holder):
        return pl.ds((block * HEAD + holder) * PIECES, PIECES)

    def columns_of(owner, head):
        return pl.ds(pl.multiple_of((owner * heads + head) * DH, DH), DH)

    def landing(t, head, block):
        if t < 2:
            return kvs[head].at[t, rows_of(block, r)]
        return qb.at[head, block]

    def local_copy(t, head):
        return pltpu.make_async_copy(
            sources[t].at[:, :, columns_of(z, head)], landing(t, head, z), local_sem.at[t, head]
        )

    def meta_copy(d, block):
        return pltpu.make_async_remote_copy(
            meta, metas.at[block], meta_send.at[d], meta_recv.at[d],
            device_id={"ctx": flipped(z, d)}, device_id_type=MESH,
        )

    def z_copy(t, head, d, block):
        peer = flipped(z, d)
        return pltpu.make_async_remote_copy(
            sources[t].at[:, :, columns_of(peer, head)], landing(t, head, block),
            z_send.at[t, head, d], z_recv.at[t, head, d],
            device_id={"ctx": peer}, device_id_type=MESH,
        )

    def row_copy(head, d, holder, peer, send, recv):
        piece = kvs[head].at[:, rows_of(flipped(z, d), holder)]
        return pltpu.make_async_remote_copy(
            piece, piece, send.at[head, d], recv.at[head, d],
            device_id={"head": peer}, device_id_type=MESH,
        )

    def x_copy(head, d, holder):
        return row_copy(head, d, holder, x_peer, x_send, x_recv)

    def own_copy(head, d, holder):
        return row_copy(head, d, holder, sibling, own_send, own_recv)

    def relay_copy(head, d, holder):
        return row_copy(head, d, holder, sibling, relay_send, relay_recv)

    side_rows = (0, ROWS)
    middle_rows = (pl.multiple_of((1 - right) * EDGE, EDGE), ROWS - EDGE)
    edge_rows = (pl.multiple_of(right * (ROWS - EDGE), EDGE), EDGE)

    def out_copy(head, d, owner, rows, send, recv):
        peer = flipped(z, d)
        where = pl.ds(*rows)
        return pltpu.make_async_remote_copy(
            ob.at[head, peer, where], out_ref.at[where, columns_of(owner, head)],
            send.at[head, d], recv.at[head, d],
            device_id={"ctx": peer}, device_id_type=MESH,
        )

    def out_local(head, rows, send):
        where = pl.ds(*rows)
        return pltpu.make_async_copy(
            ob.at[head, z, where], out_ref.at[where, columns_of(z, head)], send.at[head, 0]
        )

    for head in range(heads):
        for t in range(3):
            local_copy(t, head).start()
    meta[:COLS, :NB] = neighbors_ref[...]
    for place in range(COLS):
        row = COUNT_ROW + place
        meta[row : row + 1, :] = jnp.full((1, 128), counts_ref[place], jnp.int32)

    barrier = pltpu.get_barrier_semaphore()
    for d in range(1, CTX):
        pl.semaphore_signal(barrier, inc=1, device_id={"ctx": flipped(z, d)}, device_id_type=MESH)
    for peer in (x_peer, sibling):
        pl.semaphore_signal(barrier, inc=1, device_id={"head": peer}, device_id_type=MESH)
    pl.semaphore_wait(barrier, CTX + 1)

    for d in FAR_FIRST:
        meta_copy(d, z).start()
    def send_kv(head):
        for t in (0, 1):
            for d in FAR_FIRST:
                z_copy(t, head, d, z).start()

    def send_q(head):
        for d in FAR_FIRST:
            z_copy(2, head, d, z).start()

    send_kv(0)
    send_kv(1)
    send_q(0)
    send_kv(2)
    send_q(1)
    send_q(2)
    for head in range(heads):
        local_copy(0, head).wait()
        local_copy(1, head).wait()
        x_copy(head, 0, r).start()
        own_copy(head, 0, r).start()

    metas[z] = meta[...]
    for d in ARRIVAL:
        meta_copy(d, flipped(z, d)).wait_recv()
    to_scalars = pltpu.make_async_copy(metas, lists, lists_sem)
    to_scalars.start()
    slot = lax.broadcasted_iota(jnp.int32, (1, TILE), 1)
    for tile in range(TILES):
        row = COUNT_ROW + tile % COLS
        count = metas[tile // COLS, row : row + 1, :1]
        bias[tile] = jnp.where(slot < count, 0.0, -jnp.inf)
    to_scalars.wait()

    def forward_own(head):
        for d in ARRIVAL:
            for t in (0, 1):
                z_copy(t, head, d, flipped(z, d)).wait_recv()
            x_copy(head, d, r).start()
            own_copy(head, d, r).start()

    def forward_relay(head):
        for d in (0,) + ARRIVAL:
            x_copy(head, d, x_peer).wait_recv()
            relay_copy(head, d, x_peer).start()

    def ready(head):
        for d in (0,) + ARRIVAL:
            own_copy(head, d, sibling).wait_recv()
            relay_copy(head, d, flipped(r, 3)).wait_recv()

    side_tiles = [b * COLS + right + side for b in range(CTX) for side in range(2)]

    def await_queries(head, d):
        @pl.when(d == 0)
        def _():
            local_copy(2, head).wait()

        @pl.when(d > 0)
        def _():
            z_copy(2, head, d, flipped(z, d)).wait_recv()

    def send_out(head, d, rows, send, recv):
        @pl.when(d == 0)
        def _():
            out_local(head, rows, send).start()

        @pl.when(d > 0)
        def _():
            out_copy(head, d, z, rows, send, recv).start()

    def compute(head):
        def one(step, carry):
            d = (step + 2) % CTX
            block = flipped(z, d)
            await_queries(head, d)

            @pl.when(is_side)
            def _():
                rows = pl.ds(*side_rows)
                queries = jnp.concatenate([qb[head, block, piece] for piece in range(PIECES)], axis=0)
                ob[head, block, rows, :] = attended(queries, kvs[head], bias, side_tiles)
                send_out(head, d, side_rows, o_send, o_recv)

            @pl.when(jnp.logical_not(is_side))
            def _():
                rows = pl.ds(*middle_rows)
                tiles = [lists[block, 1, entry] for entry in range(NB)]
                queries = jnp.concatenate([qb[head, block, 1 - right + piece] for piece in range(2)], axis=0)
                ob[head, block, rows, :] = attended(queries, kvs[head], bias, tiles)
                send_out(head, d, middle_rows, o_send, o_recv)

            return carry

        lax.fori_loop(0, CTX, one, 0)

        @pl.when(jnp.logical_not(is_side))
        def _():
            rows = pl.ds(*edge_rows)
            gathered = jnp.concatenate([qb[head, block, 2 * right] for block in range(CTX)], axis=0)
            result = attended(gathered, kvs[head], bias, side_tiles)
            for block in range(CTX):
                ob[head, block, rows, :] = result[block * EDGE : (block + 1) * EDGE]
            for d in FAR_FIRST:
                out_copy(head, d, z, edge_rows, e_send, e_recv).start()
            out_local(head, edge_rows, e_send).start()

    forward_own(0)
    forward_relay(0)
    forward_own(1)
    ready(0)
    compute(0)
    forward_relay(1)
    forward_own(2)
    ready(1)
    compute(1)
    forward_relay(2)
    ready(2)
    compute(2)

    def settle(head, rows, send, recv):
        out_local(head, rows, send).wait()
        for d in ARRIVAL:
            out_copy(head, d, z, rows, send, recv).wait_send()
            out_copy(head, d, flipped(z, d), rows, send, recv).wait_recv()

    for d in ARRIVAL:
        meta_copy(d, z).wait_send()
    for head in range(heads):
        for d in range(CTX):
            x_copy(head, d, r).wait_send()
            own_copy(head, d, r).wait_send()
            relay_copy(head, d, x_peer).wait_send()
        for d in ARRIVAL:
            for t in range(3):
                z_copy(t, head, d, z).wait_send()

    @pl.when(is_side)
    def _():
        for head in range(heads):
            settle(head, side_rows, o_send, o_recv)

    @pl.when(jnp.logical_not(is_side))
    def _():
        for head in range(heads):
            settle(head, middle_rows, o_send, o_recv)
            settle(head, edge_rows, e_send, e_recv)


def clip_attention(queries, keys, values, neighbors, tile_counts):
    rows, width = queries.shape
    heads = width // DH // CTX
    anywhere = pl.BlockSpec(memory_space=pl.ANY)
    dma = pltpu.SemaphoreType.DMA
    each = dma((heads, CTX))
    queries, keys, values = (
        array.reshape(PIECES, EDGE, width) for array in (queries, keys, values)
    )
    return pl.pallas_call(
        functools.partial(clip_kernel, heads),
        out_shape=pltpu.VMEM((rows, width), queries.dtype),
        in_specs=[anywhere] * 3 + [
            pl.BlockSpec(memory_space=pltpu.VMEM), pl.BlockSpec(memory_space=pltpu.SMEM)
        ],
        out_specs=pl.BlockSpec(memory_space=pltpu.VMEM),
        scratch_shapes=[pltpu.VMEM((2, TILES * PER_TILE, EDGE, DH), keys.dtype)] * heads + [
            pltpu.VMEM((heads, CTX, PIECES, EDGE, DH), queries.dtype),
            pltpu.VMEM((heads, CTX, ROWS, DH), queries.dtype),
            pltpu.VMEM((16, 128), jnp.int32),
            pltpu.VMEM((CTX, 16, 128), jnp.int32),
            pltpu.VMEM((TILES, 1, TILE), jnp.float32),
            pltpu.SMEM((CTX, 16, 128), jnp.int32),
            dma, dma((CTX,)), dma((CTX,)),
            dma((3, heads, CTX)), dma((3, heads, CTX)), dma((3, heads)),
        ] + [each] * 10,
        compiler_params=pltpu.CompilerParams(
            collective_id=0, has_side_effects=True, vmem_limit_bytes=62 * 1024 * 1024 + 512 * 1024
        ),
    )(queries, keys, values, neighbors, tile_counts)


def shards(queries, keys, values, neighbors, tile_counts):
    rows, width = queries.shape
    whole_clip = lax.axis_size("ctx") == CTX and lax.axis_size("head") == HEAD
    if whole_clip and tile_counts.shape[0] == COLS:
        return clip_attention(queries, keys, values, neighbors, tile_counts)
    head_peers = lax.axis_size("head")
    group = width // head_peers
    paired = jnp.concatenate(
        [keys.reshape(rows, head_peers, group), values.reshape(rows, head_peers, group)], axis=2
    )
    block_kv = lax.all_to_all(paired, "head", split_axis=1, concat_axis=0, tiled=True)
    block_kv = block_kv.reshape(rows * head_peers, 2 * group)
    tiles_here = tile_counts.shape[0]
    local_heads = group // DH
    ctx_peers = lax.axis_size("ctx")
    if ctx_peers <= 2 * HOPS + 1:
        ext_tiles = ctx_peers * tiles_here
        pieces = jnp.stack([tile_counts // 16, tile_counts % 16], axis=1).astype(jnp.bfloat16)
        ext_kv, pieces = lax.all_gather((block_kv, pieces), "ctx", axis=0, tiled=True)
        pieces = pieces.astype(jnp.int32)
        ext_counts = pieces[:, 0] * 16 + pieces[:, 1]
        first_tile = 0
    else:
        earlier = []
        later = []
        for distance in range(1, HOPS + 1):
            taken = min(tiles_here, REACH - (distance - 1) * tiles_here)
            rows_taken = taken * TILE
            earlier = [shifted((block_kv[-rows_taken:], tile_counts[-taken:]), "ctx", distance)] + earlier
            later = later + [shifted((block_kv[:rows_taken], tile_counts[:taken]), "ctx", -distance)]
        ext_tiles = tiles_here + 2 * REACH
        ext_kv = jnp.concatenate([p[0] for p in earlier] + [block_kv] + [p[0] for p in later], axis=0)
        ext_counts = jnp.concatenate([p[1] for p in earlier] + [tile_counts] + [p[1] for p in later], axis=0)
        first_tile = lax.axis_index("ctx") * tiles_here - REACH
    ext_kv = ext_kv.reshape(ext_tiles, TILE, 2 * group)
    local_lists = jnp.clip(neighbors - first_tile, 0, ext_tiles - 1).astype(jnp.int32)
    block_queries = lax.all_to_all(queries, "head", split_axis=1, concat_axis=0, tiled=True)
    query_tiles = block_queries.reshape(tiles_here, TILE, group)
    outputs = attend(local_lists, ext_counts.astype(jnp.int32), query_tiles, ext_kv)
    outputs = outputs.reshape(tiles_here * TILE, group)
    return lax.all_to_all(outputs, "head", split_axis=0, concat_axis=1, tiled=True)


def solution(mesh):
    placed = (
        P(("clips", "ctx", "head"), None),
        P(("clips", "ctx", "head"), None),
        P(("clips", "ctx", "head"), None),
        P(("clips", "ctx"), None),
        P(("clips", "ctx")),
    )
    return jax.shard_map(
        shards,
        mesh=mesh,
        in_specs=placed,
        out_specs=P(("clips", "ctx", "head"), None),
        check_vma=False,
    )
```

```python
import functools

import jax
import jax.numpy as jnp
from jax import lax
from jax.sharding import PartitionSpec as P
from jax.experimental import pallas as pl
from jax.experimental.pallas import tpu as pltpu

DH = 128
TILE = 384
NB = 8
REACH = 10
HOPS = 4


def shifted(array, axis, by):
    peers = lax.axis_size(axis)
    pairs = [(i, i + by) for i in range(peers) if 0 <= i + by < peers]
    return lax.ppermute(array, axis, pairs)


def attend_kernel(lists_ref, counts_ref, query_ref, *refs):
    key_refs = refs[:NB]
    value_refs = refs[NB : 2 * NB]
    out_ref = refs[2 * NB]
    tile = pl.program_id(0)
    query_rows = query_ref[...]
    slot_index = lax.broadcasted_iota(jnp.int32, (TILE, TILE), 1)
    scores = []
    for entry in range(NB):
        part = lax.dot_general(
            query_rows, key_refs[entry][...], (((1,), (1,)), ((), ())),
            preferred_element_type=jnp.float32,
        ) * DH ** (-0.5)
        live = slot_index < counts_ref[lists_ref[tile, entry]]
        scores.append(jnp.where(live, part, -jnp.inf))
    highest = scores[0].max(axis=1, keepdims=True)
    for part in scores[1:]:
        highest = jnp.maximum(highest, part.max(axis=1, keepdims=True))
    totals = jnp.zeros((TILE, 1), jnp.float32)
    summed = jnp.zeros((TILE, DH), jnp.float32)
    for entry in range(NB):
        weights = jnp.exp(scores[entry] - highest)
        totals = totals + weights.sum(axis=1, keepdims=True)
        summed = summed + jnp.dot(
            weights.astype(jnp.bfloat16), value_refs[entry][...],
            preferred_element_type=jnp.float32,
        )
    out_ref[...] = (summed / totals).astype(out_ref.dtype)


def attend(local_lists, ext_counts, query_tiles, ext_kv):
    tiles_here, _, local_width = query_tiles.shape
    local_heads = local_width // DH
    own = pl.BlockSpec((None, TILE, DH), lambda t, h, lists, counts: (t, 0, h))

    def listed(entry, offset):
        return pl.BlockSpec(
            (None, TILE, DH), lambda t, h, lists, counts: (lists[t, entry], 0, h + offset)
        )

    spec = pltpu.PrefetchScalarGridSpec(
        num_scalar_prefetch=2,
        grid=(tiles_here, local_heads),
        in_specs=[own] + [listed(e, 0) for e in range(NB)] + [listed(e, local_heads) for e in range(NB)],
        out_specs=own,
    )
    return pl.pallas_call(
        attend_kernel,
        grid_spec=spec,
        out_shape=jax.ShapeDtypeStruct(query_tiles.shape, query_tiles.dtype),
        compiler_params=pltpu.CompilerParams(vmem_limit_bytes=48 * 1024 * 1024),
    )(local_lists, ext_counts, query_tiles, *([ext_kv] * (2 * NB)))


MESH = pl.DeviceIdType.MESH
CTX = 4
HEAD = 4
COLS = 3
ROWS = COLS * TILE // HEAD
EDGE = TILE - ROWS
PIECES = ROWS // EDGE
PER_TILE = TILE // EDGE
BLOCK = COLS * TILE
SLOTS = CTX * BLOCK
TILES = CTX * COLS
COUNT_ROW = 8
EXP2_SCALE = DH ** (-0.5) * 1.4426950408889634
FAR_FIRST = (2, 3, 1)
ARRIVAL = (1, 2, 3)


def flipped(index, by):
    high = (index // 2 + by // 2) % 2
    low = (index % 2 + by % 2) % 2
    return 2 * high + low


def attended(query_rows, kv, bias, tiles):
    def rows_of(side, tile):
        return jnp.concatenate([kv[side, tile * PER_TILE + piece] for piece in range(PER_TILE)], axis=0)

    scores = []
    highest = None
    for tile in tiles:
        part = lax.dot_general(
            query_rows, rows_of(0, tile), (((1,), (1,)), ((), ())), preferred_element_type=jnp.float32
        ) + bias[tile]
        scores.append(part)
        top = part.max(axis=1, keepdims=True)
        highest = top if highest is None else jnp.maximum(highest, top)
    totals = jnp.zeros_like(highest)
    summed = jnp.zeros((query_rows.shape[0], DH), jnp.float32)
    for part, tile in zip(scores, tiles):
        weights = jnp.exp2((part - highest) * EXP2_SCALE)
        totals = totals + weights.sum(axis=1, keepdims=True)
        summed = summed + jnp.dot(
            weights.astype(jnp.bfloat16), rows_of(1, tile), preferred_element_type=jnp.float32
        )
    return (summed / totals).astype(query_rows.dtype)


def clip_kernel(
    heads, q_hbm, k_hbm, v_hbm, neighbors_ref, counts_ref, out_ref, *refs
):
    kvs = refs[:heads]
    (
        qb, ob, meta, metas, bias, lists,
        lists_sem, meta_send, meta_recv, z_send, z_recv, local_sem,
        x_send, x_recv, own_send, own_recv, relay_send, relay_recv,
        o_send, o_recv, e_send, e_recv,
    ) = refs[heads:]
    z = lax.axis_index("ctx")
    r = lax.axis_index("head")
    x_peer = (r + 2) % HEAD
    sibling = flipped(r, 1)
    right = r // 2
    is_side = (r == 0) | (r == HEAD - 1)
    sources = (k_hbm, v_hbm, q_hbm)

    def rows_of(block, holder):
        return pl.ds((block * HEAD + holder) * PIECES, PIECES)

    def columns_of(owner, head):
        return pl.ds(pl.multiple_of((owner * heads + head) * DH, DH), DH)

    def landing(t, head, block):
        if t < 2:
            return kvs[head].at[t, rows_of(block, r)]
        return qb.at[head, block]

    def local_copy(t, head):
        return pltpu.make_async_copy(
            sources[t].at[:, :, columns_of(z, head)], landing(t, head, z), local_sem.at[t, head]
        )

    def meta_copy(d, block):
        return pltpu.make_async_remote_copy(
            meta, metas.at[block], meta_send.at[d], meta_recv.at[d],
            device_id={"ctx": flipped(z, d)}, device_id_type=MESH,
        )

    def z_copy(t, head, d, block):
        peer = flipped(z, d)
        return pltpu.make_async_remote_copy(
            sources[t].at[:, :, columns_of(peer, head)], landing(t, head, block),
            z_send.at[t, head, d], z_recv.at[t, head, d],
            device_id={"ctx": peer}, device_id_type=MESH,
        )

    def row_copy(head, d, holder, peer, send, recv):
        piece = kvs[head].at[:, rows_of(flipped(z, d), holder)]
        return pltpu.make_async_remote_copy(
            piece, piece, send.at[head, d], recv.at[head, d],
            device_id={"head": peer}, device_id_type=MESH,
        )

    def x_copy(head, d, holder):
        return row_copy(head, d, holder, x_peer, x_send, x_recv)

    def own_copy(head, d, holder):
        return row_copy(head, d, holder, sibling, own_send, own_recv)

    def relay_copy(head, d, holder):
        return row_copy(head, d, holder, sibling, relay_send, relay_recv)

    side_rows = (0, ROWS)
    middle_rows = (pl.multiple_of((1 - right) * EDGE, EDGE), ROWS - EDGE)
    edge_rows = (pl.multiple_of(right * (ROWS - EDGE), EDGE), EDGE)

    def out_copy(head, d, owner, rows, send, recv):
        peer = flipped(z, d)
        where = pl.ds(*rows)
        return pltpu.make_async_remote_copy(
            ob.at[head, peer, where], out_ref.at[where, columns_of(owner, head)],
            send.at[head, d], recv.at[head, d],
            device_id={"ctx": peer}, device_id_type=MESH,
        )

    def out_local(head, rows, send):
        where = pl.ds(*rows)
        return pltpu.make_async_copy(
            ob.at[head, z, where], out_ref.at[where, columns_of(z, head)], send.at[head, 0]
        )

    meta[:COLS, :NB] = neighbors_ref[...]
    for place in range(COLS):
        row = COUNT_ROW + place
        meta[row : row + 1, :] = jnp.full((1, 128), counts_ref[place], jnp.int32)

    barrier = pltpu.get_barrier_semaphore()
    for d in range(1, CTX):
        pl.semaphore_signal(barrier, inc=1, device_id={"ctx": flipped(z, d)}, device_id_type=MESH)
    for peer in (x_peer, sibling):
        pl.semaphore_signal(barrier, inc=1, device_id={"head": peer}, device_id_type=MESH)
    pl.semaphore_wait(barrier, CTX + 1)

    inner = (z % 2 + z // 2) % 2
    order = (3 - 2 * inner, 2, 1 + 2 * inner)

    def send_kv(head):
        for t in (0, 1):
            for d in order:
                z_copy(t, head, d, z).start()

    def send_q(head):
        for d in order:
            z_copy(2, head, d, z).start()

    send_kv(0)
    for d in FAR_FIRST:
        meta_copy(d, z).start()
    for head in range(heads):
        for t in range(3):
            local_copy(t, head).start()
    send_kv(1)
    send_q(0)
    send_kv(2)
    send_q(1)
    send_q(2)
    for head in range(heads):
        local_copy(0, head).wait()
        local_copy(1, head).wait()
        x_copy(head, 0, r).start()
        own_copy(head, 0, r).start()

    metas[z] = meta[...]
    for d in ARRIVAL:
        meta_copy(d, flipped(z, d)).wait_recv()
    to_scalars = pltpu.make_async_copy(metas, lists, lists_sem)
    to_scalars.start()
    slot = lax.broadcasted_iota(jnp.int32, (1, TILE), 1)
    for tile in range(TILES):
        row = COUNT_ROW + tile % COLS
        count = metas[tile // COLS, row : row + 1, :1]
        bias[tile] = jnp.where(slot < count, 0.0, -jnp.inf)
    to_scalars.wait()

    def forward_own(head):
        for d in ARRIVAL:
            for t in (0, 1):
                z_copy(t, head, d, flipped(z, d)).wait_recv()
            x_copy(head, d, r).start()
            own_copy(head, d, r).start()

    def forward_relay(head):
        for d in (0,) + ARRIVAL:
            x_copy(head, d, x_peer).wait_recv()
            relay_copy(head, d, x_peer).start()

    def ready(head):
        for d in (0,) + ARRIVAL:
            own_copy(head, d, sibling).wait_recv()
            relay_copy(head, d, flipped(r, 3)).wait_recv()

    side_tiles = [b * COLS + right + side for b in range(CTX) for side in range(2)]

    def await_queries(head, d):
        @pl.when(d == 0)
        def _():
            local_copy(2, head).wait()

        @pl.when(d > 0)
        def _():
            z_copy(2, head, d, flipped(z, d)).wait_recv()

    def send_out(head, d, rows, send, recv):
        @pl.when(d == 0)
        def _():
            out_local(head, rows, send).start()

        @pl.when(d > 0)
        def _():
            out_copy(head, d, z, rows, send, recv).start()

    def compute(head):
        def one(step, carry):
            d = (step + 2) % CTX
            block = flipped(z, d)
            await_queries(head, d)

            @pl.when(is_side)
            def _():
                rows = pl.ds(*side_rows)
                queries = jnp.concatenate([qb[head, block, piece] for piece in range(PIECES)], axis=0)
                ob[head, block, rows, :] = attended(queries, kvs[head], bias, side_tiles)
                send_out(head, d, side_rows, o_send, o_recv)

            @pl.when(jnp.logical_not(is_side))
            def _():
                rows = pl.ds(*middle_rows)
                tiles = [lists[block, 1, entry] for entry in range(NB)]
                queries = jnp.concatenate([qb[head, block, 1 - right + piece] for piece in range(2)], axis=0)
                ob[head, block, rows, :] = attended(queries, kvs[head], bias, tiles)
                send_out(head, d, middle_rows, o_send, o_recv)

            return carry

        lax.fori_loop(0, CTX, one, 0)

        @pl.when(jnp.logical_not(is_side))
        def _():
            rows = pl.ds(*edge_rows)
            gathered = jnp.concatenate([qb[head, block, 2 * right] for block in range(CTX)], axis=0)
            result = attended(gathered, kvs[head], bias, side_tiles)
            for block in range(CTX):
                ob[head, block, rows, :] = result[block * EDGE : (block + 1) * EDGE]
            for d in FAR_FIRST:
                out_copy(head, d, z, edge_rows, e_send, e_recv).start()
            out_local(head, edge_rows, e_send).start()

    forward_own(0)
    forward_relay(0)
    forward_own(1)
    ready(0)
    compute(0)
    forward_relay(1)
    forward_own(2)
    ready(1)
    compute(1)
    forward_relay(2)
    ready(2)
    compute(2)

    def settle(head, rows, send, recv):
        out_local(head, rows, send).wait()
        for d in ARRIVAL:
            out_copy(head, d, z, rows, send, recv).wait_send()
            out_copy(head, d, flipped(z, d), rows, send, recv).wait_recv()

    for d in ARRIVAL:
        meta_copy(d, z).wait_send()
    for head in range(heads):
        for d in range(CTX):
            x_copy(head, d, r).wait_send()
            own_copy(head, d, r).wait_send()
            relay_copy(head, d, x_peer).wait_send()
        for d in ARRIVAL:
            for t in range(3):
                z_copy(t, head, d, z).wait_send()

    @pl.when(is_side)
    def _():
        for head in range(heads):
            settle(head, side_rows, o_send, o_recv)

    @pl.when(jnp.logical_not(is_side))
    def _():
        for head in range(heads):
            settle(head, middle_rows, o_send, o_recv)
            settle(head, edge_rows, e_send, e_recv)


def clip_attention(queries, keys, values, neighbors, tile_counts):
    rows, width = queries.shape
    heads = width // DH // CTX
    anywhere = pl.BlockSpec(memory_space=pl.ANY)
    dma = pltpu.SemaphoreType.DMA
    each = dma((heads, CTX))
    queries, keys, values = (
        array.reshape(PIECES, EDGE, width) for array in (queries, keys, values)
    )
    return pl.pallas_call(
        functools.partial(clip_kernel, heads),
        out_shape=pltpu.VMEM((rows, width), queries.dtype),
        in_specs=[anywhere] * 3 + [
            pl.BlockSpec(memory_space=pltpu.VMEM), pl.BlockSpec(memory_space=pltpu.SMEM)
        ],
        out_specs=pl.BlockSpec(memory_space=pltpu.VMEM),
        scratch_shapes=[pltpu.VMEM((2, TILES * PER_TILE, EDGE, DH), keys.dtype)] * heads + [
            pltpu.VMEM((heads, CTX, PIECES, EDGE, DH), queries.dtype),
            pltpu.VMEM((heads, CTX, ROWS, DH), queries.dtype),
            pltpu.VMEM((16, 128), jnp.int32),
            pltpu.VMEM((CTX, 16, 128), jnp.int32),
            pltpu.VMEM((TILES, 1, TILE), jnp.float32),
            pltpu.SMEM((CTX, 16, 128), jnp.int32),
            dma, dma((CTX,)), dma((CTX,)),
            dma((3, heads, CTX)), dma((3, heads, CTX)), dma((3, heads)),
        ] + [each] * 10,
        compiler_params=pltpu.CompilerParams(
            collective_id=0, has_side_effects=True, vmem_limit_bytes=62 * 1024 * 1024 + 512 * 1024
        ),
    )(queries, keys, values, neighbors, tile_counts)


def shards(queries, keys, values, neighbors, tile_counts):
    rows, width = queries.shape
    whole_clip = lax.axis_size("ctx") == CTX and lax.axis_size("head") == HEAD
    if whole_clip and tile_counts.shape[0] == COLS:
        return clip_attention(queries, keys, values, neighbors, tile_counts)
    head_peers = lax.axis_size("head")
    group = width // head_peers
    paired = jnp.concatenate(
        [keys.reshape(rows, head_peers, group), values.reshape(rows, head_peers, group)], axis=2
    )
    block_kv = lax.all_to_all(paired, "head", split_axis=1, concat_axis=0, tiled=True)
    block_kv = block_kv.reshape(rows * head_peers, 2 * group)
    tiles_here = tile_counts.shape[0]
    local_heads = group // DH
    ctx_peers = lax.axis_size("ctx")
    if ctx_peers <= 2 * HOPS + 1:
        ext_tiles = ctx_peers * tiles_here
        pieces = jnp.stack([tile_counts // 16, tile_counts % 16], axis=1).astype(jnp.bfloat16)
        ext_kv, pieces = lax.all_gather((block_kv, pieces), "ctx", axis=0, tiled=True)
        pieces = pieces.astype(jnp.int32)
        ext_counts = pieces[:, 0] * 16 + pieces[:, 1]
        first_tile = 0
    else:
        earlier = []
        later = []
        for distance in range(1, HOPS + 1):
            taken = min(tiles_here, REACH - (distance - 1) * tiles_here)
            rows_taken = taken * TILE
            earlier = [shifted((block_kv[-rows_taken:], tile_counts[-taken:]), "ctx", distance)] + earlier
            later = later + [shifted((block_kv[:rows_taken], tile_counts[:taken]), "ctx", -distance)]
        ext_tiles = tiles_here + 2 * REACH
        ext_kv = jnp.concatenate([p[0] for p in earlier] + [block_kv] + [p[0] for p in later], axis=0)
        ext_counts = jnp.concatenate([p[1] for p in earlier] + [tile_counts] + [p[1] for p in later], axis=0)
        first_tile = lax.axis_index("ctx") * tiles_here - REACH
    ext_kv = ext_kv.reshape(ext_tiles, TILE, 2 * group)
    local_lists = jnp.clip(neighbors - first_tile, 0, ext_tiles - 1).astype(jnp.int32)
    block_queries = lax.all_to_all(queries, "head", split_axis=1, concat_axis=0, tiled=True)
    query_tiles = block_queries.reshape(tiles_here, TILE, group)
    outputs = attend(local_lists, ext_counts.astype(jnp.int32), query_tiles, ext_kv)
    outputs = outputs.reshape(tiles_here * TILE, group)
    return lax.all_to_all(outputs, "head", split_axis=0, concat_axis=1, tiled=True)


def solution(mesh):
    placed = (
        P(("clips", "ctx", "head"), None),
        P(("clips", "ctx", "head"), None),
        P(("clips", "ctx", "head"), None),
        P(("clips", "ctx"), None),
        P(("clips", "ctx")),
    )
    return jax.shard_map(
        shards,
        mesh=mesh,
        in_specs=placed,
        out_specs=P(("clips", "ctx", "head"), None),
        check_vma=False,
    )
```

```python
import functools

import jax
import jax.numpy as jnp
from jax import lax
from jax.sharding import PartitionSpec as P
from jax.experimental import pallas as pl
from jax.experimental.pallas import tpu as pltpu

DH = 128
TILE = 384
NB = 8
REACH = 10
HOPS = 4


def shifted(array, axis, by):
    peers = lax.axis_size(axis)
    pairs = [(i, i + by) for i in range(peers) if 0 <= i + by < peers]
    return lax.ppermute(array, axis, pairs)


def attend_kernel(lists_ref, counts_ref, query_ref, *refs):
    key_refs = refs[:NB]
    value_refs = refs[NB : 2 * NB]
    out_ref = refs[2 * NB]
    tile = pl.program_id(0)
    query_rows = query_ref[...]
    slot_index = lax.broadcasted_iota(jnp.int32, (TILE, TILE), 1)
    scores = []
    for entry in range(NB):
        part = lax.dot_general(
            query_rows, key_refs[entry][...], (((1,), (1,)), ((), ())),
            preferred_element_type=jnp.float32,
        ) * DH ** (-0.5)
        live = slot_index < counts_ref[lists_ref[tile, entry]]
        scores.append(jnp.where(live, part, -jnp.inf))
    highest = scores[0].max(axis=1, keepdims=True)
    for part in scores[1:]:
        highest = jnp.maximum(highest, part.max(axis=1, keepdims=True))
    totals = jnp.zeros((TILE, 1), jnp.float32)
    summed = jnp.zeros((TILE, DH), jnp.float32)
    for entry in range(NB):
        weights = jnp.exp(scores[entry] - highest)
        totals = totals + weights.sum(axis=1, keepdims=True)
        summed = summed + jnp.dot(
            weights.astype(jnp.bfloat16), value_refs[entry][...],
            preferred_element_type=jnp.float32,
        )
    out_ref[...] = (summed / totals).astype(out_ref.dtype)


def attend(local_lists, ext_counts, query_tiles, ext_kv):
    tiles_here, _, local_width = query_tiles.shape
    local_heads = local_width // DH
    own = pl.BlockSpec((None, TILE, DH), lambda t, h, lists, counts: (t, 0, h))

    def listed(entry, offset):
        return pl.BlockSpec(
            (None, TILE, DH), lambda t, h, lists, counts: (lists[t, entry], 0, h + offset)
        )

    spec = pltpu.PrefetchScalarGridSpec(
        num_scalar_prefetch=2,
        grid=(tiles_here, local_heads),
        in_specs=[own] + [listed(e, 0) for e in range(NB)] + [listed(e, local_heads) for e in range(NB)],
        out_specs=own,
    )
    return pl.pallas_call(
        attend_kernel,
        grid_spec=spec,
        out_shape=jax.ShapeDtypeStruct(query_tiles.shape, query_tiles.dtype),
        compiler_params=pltpu.CompilerParams(vmem_limit_bytes=48 * 1024 * 1024),
    )(local_lists, ext_counts, query_tiles, *([ext_kv] * (2 * NB)))


MESH = pl.DeviceIdType.MESH
CTX = 4
HEAD = 4
COLS = 3
ROWS = COLS * TILE // HEAD
EDGE = TILE - ROWS
PIECES = ROWS // EDGE
PER_TILE = TILE // EDGE
BLOCK = COLS * TILE
SLOTS = CTX * BLOCK
TILES = CTX * COLS
COUNT_ROW = 8
EXP2_SCALE = DH ** (-0.5) * 1.4426950408889634
FAR_FIRST = (2, 3, 1)
ARRIVAL = (1, 3, 2)


def flipped(index, by):
    high = (index // 2 + by // 2) % 2
    low = (index % 2 + by % 2) % 2
    return 2 * high + low


def attended(query_rows, kv, bias, tiles):
    def rows_of(side, tile):
        return jnp.concatenate([kv[side, tile * PER_TILE + piece] for piece in range(PER_TILE)], axis=0)

    scores = []
    highest = None
    for tile in tiles:
        part = lax.dot_general(
            query_rows, rows_of(0, tile), (((1,), (1,)), ((), ())), preferred_element_type=jnp.float32
        ) + bias[tile]
        scores.append(part)
        top = part.max(axis=1, keepdims=True)
        highest = top if highest is None else jnp.maximum(highest, top)
    totals = jnp.zeros_like(highest)
    summed = jnp.zeros((query_rows.shape[0], DH), jnp.float32)
    for part, tile in zip(scores, tiles):
        weights = jnp.exp2((part - highest) * EXP2_SCALE)
        totals = totals + weights.sum(axis=1, keepdims=True)
        summed = summed + jnp.dot(
            weights.astype(jnp.bfloat16), rows_of(1, tile), preferred_element_type=jnp.float32
        )
    return (summed / totals).astype(query_rows.dtype)


def clip_kernel(
    heads, q_hbm, k_hbm, v_hbm, neighbors_ref, counts_ref, out_ref, *refs
):
    kvs = refs[:heads]
    (
        qb, ob, meta, metas, bias, lists,
        lists_sem, meta_send, meta_recv, z_send, z_recv, local_sem,
        x_send, x_recv, own_send, own_recv, relay_send, relay_recv,
        o_send, o_recv, e_send, e_recv,
    ) = refs[heads:]
    z = lax.axis_index("ctx")
    r = lax.axis_index("head")
    x_peer = (r + 2) % HEAD
    sibling = flipped(r, 1)
    right = r // 2
    is_side = (r == 0) | (r == HEAD - 1)
    sources = (k_hbm, v_hbm, q_hbm)

    def rows_of(block, holder):
        return pl.ds((block * HEAD + holder) * PIECES, PIECES)

    def columns_of(owner, head):
        return pl.ds(pl.multiple_of((owner * heads + head) * DH, DH), DH)

    def landing(t, head, block):
        if t < 2:
            return kvs[head].at[t, rows_of(block, r)]
        return qb.at[head, block]

    def local_copy(t, head):
        return pltpu.make_async_copy(
            sources[t].at[:, :, columns_of(z, head)], landing(t, head, z), local_sem.at[t, head]
        )

    def meta_copy(d, block):
        return pltpu.make_async_remote_copy(
            meta, metas.at[block], meta_send.at[d], meta_recv.at[d],
            device_id={"ctx": flipped(z, d)}, device_id_type=MESH,
        )

    def z_copy(t, head, d, block):
        peer = flipped(z, d)
        return pltpu.make_async_remote_copy(
            sources[t].at[:, :, columns_of(peer, head)], landing(t, head, block),
            z_send.at[t, head, d], z_recv.at[t, head, d],
            device_id={"ctx": peer}, device_id_type=MESH,
        )

    def row_copy(head, d, holder, peer, send, recv):
        piece = kvs[head].at[:, rows_of(flipped(z, d), holder)]
        return pltpu.make_async_remote_copy(
            piece, piece, send.at[head, d], recv.at[head, d],
            device_id={"head": peer}, device_id_type=MESH,
        )

    def x_copy(head, d, holder):
        return row_copy(head, d, holder, x_peer, x_send, x_recv)

    def own_copy(head, d, holder):
        return row_copy(head, d, holder, sibling, own_send, own_recv)

    def relay_copy(head, d, holder):
        return row_copy(head, d, holder, sibling, relay_send, relay_recv)

    side_rows = (0, ROWS)
    middle_rows = (pl.multiple_of((1 - right) * EDGE, EDGE), ROWS - EDGE)
    edge_rows = (pl.multiple_of(right * (ROWS - EDGE), EDGE), EDGE)

    def out_copy(head, d, owner, rows, send, recv):
        peer = flipped(z, d)
        where = pl.ds(*rows)
        return pltpu.make_async_remote_copy(
            ob.at[head, peer, where], out_ref.at[where, columns_of(owner, head)],
            send.at[head, d], recv.at[head, d],
            device_id={"ctx": peer}, device_id_type=MESH,
        )

    def out_local(head, rows, send):
        where = pl.ds(*rows)
        return pltpu.make_async_copy(
            ob.at[head, z, where], out_ref.at[where, columns_of(z, head)], send.at[head, 0]
        )

    for head in range(heads):
        for t in range(3):
            local_copy(t, head).start()
    meta[:COLS, :NB] = neighbors_ref[...]
    for place in range(COLS):
        row = COUNT_ROW + place
        meta[row : row + 1, :] = jnp.full((1, 128), counts_ref[place], jnp.int32)

    barrier = pltpu.get_barrier_semaphore()
    for d in range(1, CTX):
        pl.semaphore_signal(barrier, inc=1, device_id={"ctx": flipped(z, d)}, device_id_type=MESH)
    for peer in (x_peer, sibling):
        pl.semaphore_signal(barrier, inc=1, device_id={"head": peer}, device_id_type=MESH)
    pl.semaphore_wait(barrier, CTX + 1)

    for d in FAR_FIRST:
        meta_copy(d, z).start()
    def send_kv(head):
        for t in (0, 1):
            for d in FAR_FIRST:
                z_copy(t, head, d, z).start()

    def send_q(head):
        for d in FAR_FIRST:
            z_copy(2, head, d, z).start()

    send_kv(0)
    send_kv(1)
    send_q(0)
    send_kv(2)
    send_q(1)
    send_q(2)
    for head in range(heads):
        local_copy(0, head).wait()
        local_copy(1, head).wait()
        x_copy(head, 0, r).start()
        own_copy(head, 0, r).start()

    metas[z] = meta[...]
    for d in ARRIVAL:
        meta_copy(d, flipped(z, d)).wait_recv()
    to_scalars = pltpu.make_async_copy(metas, lists, lists_sem)
    to_scalars.start()
    slot = lax.broadcasted_iota(jnp.int32, (1, TILE), 1)
    for tile in range(TILES):
        row = COUNT_ROW + tile % COLS
        count = metas[tile // COLS, row : row + 1, :1]
        bias[tile] = jnp.where(slot < count, 0.0, -jnp.inf)
    to_scalars.wait()

    def forward_own(head):
        for d in ARRIVAL:
            for t in (0, 1):
                z_copy(t, head, d, flipped(z, d)).wait_recv()
            x_copy(head, d, r).start()
            own_copy(head, d, r).start()

    def forward_relay(head):
        for d in (0,) + ARRIVAL:
            x_copy(head, d, x_peer).wait_recv()
            relay_copy(head, d, x_peer).start()

    def ready(head):
        for d in (0,) + ARRIVAL:
            own_copy(head, d, sibling).wait_recv()
            relay_copy(head, d, flipped(r, 3)).wait_recv()

    side_tiles = [b * COLS + right + side for b in range(CTX) for side in range(2)]

    def await_queries(head, d):
        @pl.when(d == 0)
        def _():
            local_copy(2, head).wait()

        @pl.when(d > 0)
        def _():
            z_copy(2, head, d, flipped(z, d)).wait_recv()

    def send_out(head, d, rows, send, recv):
        @pl.when(d == 0)
        def _():
            out_local(head, rows, send).start()

        @pl.when(d > 0)
        def _():
            out_copy(head, d, z, rows, send, recv).start()

    def compute(head):
        def one(step, carry):
            d = (step + 2) % CTX
            block = flipped(z, d)
            await_queries(head, d)

            @pl.when(is_side)
            def _():
                rows = pl.ds(*side_rows)
                queries = jnp.concatenate([qb[head, block, piece] for piece in range(PIECES)], axis=0)
                ob[head, block, rows, :] = attended(queries, kvs[head], bias, side_tiles)
                send_out(head, d, side_rows, o_send, o_recv)

            @pl.when(jnp.logical_not(is_side))
            def _():
                rows = pl.ds(*middle_rows)
                tiles = [lists[block, 1, entry] for entry in range(NB)]
                queries = jnp.concatenate([qb[head, block, 1 - right + piece] for piece in range(2)], axis=0)
                ob[head, block, rows, :] = attended(queries, kvs[head], bias, tiles)
                send_out(head, d, middle_rows, o_send, o_recv)

            return carry

        lax.fori_loop(0, CTX, one, 0)

        @pl.when(jnp.logical_not(is_side))
        def _():
            rows = pl.ds(*edge_rows)
            gathered = jnp.concatenate([qb[head, block, 2 * right] for block in range(CTX)], axis=0)
            result = attended(gathered, kvs[head], bias, side_tiles)
            for block in range(CTX):
                ob[head, block, rows, :] = result[block * EDGE : (block + 1) * EDGE]
            for d in FAR_FIRST:
                out_copy(head, d, z, edge_rows, e_send, e_recv).start()
            out_local(head, edge_rows, e_send).start()

    forward_own(0)
    forward_relay(0)
    forward_own(1)
    ready(0)
    compute(0)
    forward_relay(1)
    forward_own(2)
    ready(1)
    compute(1)
    forward_relay(2)
    ready(2)
    compute(2)

    def settle(head, rows, send, recv):
        out_local(head, rows, send).wait()
        for d in ARRIVAL:
            out_copy(head, d, z, rows, send, recv).wait_send()
            out_copy(head, d, flipped(z, d), rows, send, recv).wait_recv()

    for d in ARRIVAL:
        meta_copy(d, z).wait_send()
    for head in range(heads):
        for d in range(CTX):
            x_copy(head, d, r).wait_send()
            own_copy(head, d, r).wait_send()
            relay_copy(head, d, x_peer).wait_send()
        for d in ARRIVAL:
            for t in range(3):
                z_copy(t, head, d, z).wait_send()

    @pl.when(is_side)
    def _():
        for head in range(heads):
            settle(head, side_rows, o_send, o_recv)

    @pl.when(jnp.logical_not(is_side))
    def _():
        for head in range(heads):
            settle(head, middle_rows, o_send, o_recv)
            settle(head, edge_rows, e_send, e_recv)


def clip_attention(queries, keys, values, neighbors, tile_counts):
    rows, width = queries.shape
    heads = width // DH // CTX
    anywhere = pl.BlockSpec(memory_space=pl.ANY)
    dma = pltpu.SemaphoreType.DMA
    each = dma((heads, CTX))
    queries, keys, values = (
        array.reshape(PIECES, EDGE, width) for array in (queries, keys, values)
    )
    return pl.pallas_call(
        functools.partial(clip_kernel, heads),
        out_shape=pltpu.VMEM((rows, width), queries.dtype),
        in_specs=[anywhere] * 3 + [
            pl.BlockSpec(memory_space=pltpu.VMEM), pl.BlockSpec(memory_space=pltpu.SMEM)
        ],
        out_specs=pl.BlockSpec(memory_space=pltpu.VMEM),
        scratch_shapes=[pltpu.VMEM((2, TILES * PER_TILE, EDGE, DH), keys.dtype)] * heads + [
            pltpu.VMEM((heads, CTX, PIECES, EDGE, DH), queries.dtype),
            pltpu.VMEM((heads, CTX, ROWS, DH), queries.dtype),
            pltpu.VMEM((16, 128), jnp.int32),
            pltpu.VMEM((CTX, 16, 128), jnp.int32),
            pltpu.VMEM((TILES, 1, TILE), jnp.float32),
            pltpu.SMEM((CTX, 16, 128), jnp.int32),
            dma, dma((CTX,)), dma((CTX,)),
            dma((3, heads, CTX)), dma((3, heads, CTX)), dma((3, heads)),
        ] + [each] * 10,
        compiler_params=pltpu.CompilerParams(
            collective_id=0, has_side_effects=True, vmem_limit_bytes=62 * 1024 * 1024 + 512 * 1024
        ),
    )(queries, keys, values, neighbors, tile_counts)


def shards(queries, keys, values, neighbors, tile_counts):
    rows, width = queries.shape
    whole_clip = lax.axis_size("ctx") == CTX and lax.axis_size("head") == HEAD
    if whole_clip and tile_counts.shape[0] == COLS:
        return clip_attention(queries, keys, values, neighbors, tile_counts)
    head_peers = lax.axis_size("head")
    group = width // head_peers
    paired = jnp.concatenate(
        [keys.reshape(rows, head_peers, group), values.reshape(rows, head_peers, group)], axis=2
    )
    block_kv = lax.all_to_all(paired, "head", split_axis=1, concat_axis=0, tiled=True)
    block_kv = block_kv.reshape(rows * head_peers, 2 * group)
    tiles_here = tile_counts.shape[0]
    local_heads = group // DH
    ctx_peers = lax.axis_size("ctx")
    if ctx_peers <= 2 * HOPS + 1:
        ext_tiles = ctx_peers * tiles_here
        pieces = jnp.stack([tile_counts // 16, tile_counts % 16], axis=1).astype(jnp.bfloat16)
        ext_kv, pieces = lax.all_gather((block_kv, pieces), "ctx", axis=0, tiled=True)
        pieces = pieces.astype(jnp.int32)
        ext_counts = pieces[:, 0] * 16 + pieces[:, 1]
        first_tile = 0
    else:
        earlier = []
        later = []
        for distance in range(1, HOPS + 1):
            taken = min(tiles_here, REACH - (distance - 1) * tiles_here)
            rows_taken = taken * TILE
            earlier = [shifted((block_kv[-rows_taken:], tile_counts[-taken:]), "ctx", distance)] + earlier
            later = later + [shifted((block_kv[:rows_taken], tile_counts[:taken]), "ctx", -distance)]
        ext_tiles = tiles_here + 2 * REACH
        ext_kv = jnp.concatenate([p[0] for p in earlier] + [block_kv] + [p[0] for p in later], axis=0)
        ext_counts = jnp.concatenate([p[1] for p in earlier] + [tile_counts] + [p[1] for p in later], axis=0)
        first_tile = lax.axis_index("ctx") * tiles_here - REACH
    ext_kv = ext_kv.reshape(ext_tiles, TILE, 2 * group)
    local_lists = jnp.clip(neighbors - first_tile, 0, ext_tiles - 1).astype(jnp.int32)
    block_queries = lax.all_to_all(queries, "head", split_axis=1, concat_axis=0, tiled=True)
    query_tiles = block_queries.reshape(tiles_here, TILE, group)
    outputs = attend(local_lists, ext_counts.astype(jnp.int32), query_tiles, ext_kv)
    outputs = outputs.reshape(tiles_here * TILE, group)
    return lax.all_to_all(outputs, "head", split_axis=0, concat_axis=1, tiled=True)


def solution(mesh):
    placed = (
        P(("clips", "ctx", "head"), None),
        P(("clips", "ctx", "head"), None),
        P(("clips", "ctx", "head"), None),
        P(("clips", "ctx"), None),
        P(("clips", "ctx")),
    )
    return jax.shard_map(
        shards,
        mesh=mesh,
        in_specs=placed,
        out_specs=P(("clips", "ctx", "head"), None),
        check_vma=False,
    )
```
